256 devices in a mesh: gx: 4 (over x), gy: 8 (over y, core), gz: 8 (over z).
Axes of the slice: x: 4, y: 4, z: 8, core: 2. Of those that a mesh axis runs over, the one named last changes fastest.
Arguments:
- right_side: float32 [64, 256, 1024], P('gx', 'gy', 'gz'), may hold values from -8 to 8
- diagonal: float32 [64, 256, 1024], P('gx', 'gy', 'gz'), may hold values from 0.16 to 6.1
Outputs:
- solution_field: float32 [64, 256, 1024], P('gx', 'gy', 'gz')
- residual: float32 [64, 256, 1024], P('gx', 'gy', 'gz')
The draws below stay inside these ranges and needn't reach their ends.
All inputs are finite; a program needn't handle non-finite values.
Results may differ from the reference program's by a relative error of at most 0.0003.
Values sent between devices are 32-bit elements; how exact they have to be, the bound alone decides.
No kernel may reach another device: no remote copies, remote signals or barrier semaphores. Data moves between devices by JAX's collectives and lax.ppermute only.
A program may use at most 128 MiB of HBM per device.

```python
import math
import jax
import jax.numpy as jnp

ITERS = 2
NX = 64
NY = 256
NZ = 1024


def draw_right_side(key, part):
    noise = jax.random.normal(jax.random.fold_in(key, 11), (NX, NY, NZ), jnp.float32)
    values = noise
    return jnp.clip(values, -8.0, 8.0).astype(jnp.float32)


def draw_diagonal(key, part):
    logs = jax.random.uniform(jax.random.fold_in(key, 23), (NX, NY, NZ), jnp.float32, math.log(0.5), math.log(2.0))
    base = jnp.exp(logs)
    place = (jnp.arange(NZ, dtype=jnp.float32) + 0.5) / NZ
    factor = jnp.exp(math.log(3.0) * (2.0 * place - 1.0))
    return (base * factor[None, None, :]).astype(jnp.float32)


def setup_inputs(seed: int = 0) -> dict:
    keys = jax.random.split(jax.random.key(seed), 3)
    right_side = draw_right_side(jax.random.fold_in(keys[2], 71), 0)
    diagonal = draw_diagonal(jax.random.fold_in(keys[2], 71), 0)
    return dict(right_side=right_side, diagonal=diagonal)


def box_sum(padded):
    total = padded[:-2] + padded[1:-1] + padded[2:]
    total = total[:, :-2] + total[:, 1:-1] + total[:, 2:]
    return total[:, :, :-2] + total[:, :, 1:-1] + total[:, :, 2:]


def operate(field, extra):
    return (27.0 + extra) * field - box_sum(jnp.pad(field, 1))


def smooth(rhs, extra, degree, lower):
    upper = 58.0
    theta = (upper + lower) / 2.0
    delta = (upper - lower) / 2.0
    sigma = theta / delta
    rho = 1.0 / sigma
    step = rhs / theta
    total = step
    remain = rhs
    for count in range(degree - 1):
        remain = remain - operate(step, extra)
        rho_next = 1.0 / (2.0 * sigma - rho)
        step = (rho_next * rho) * step + (2.0 * rho_next / delta) * remain
        total = total + step
        rho = rho_next
    return total


def blocks(field):
    a, b, c = field.shape
    return field.reshape(a // 2, 2, b // 2, 2, c // 2, 2)


def restrict(field):
    return 0.5 * blocks(field).sum(axis=(1, 3, 5))


def prolong(field):
    a, b, c = field.shape
    wide = jnp.broadcast_to(field[:, None, :, None, :, None], (a, 2, b, 2, c, 2))
    return wide.reshape(2 * a, 2 * b, 2 * c)


def coarse(r_two, extra_two):
    solved = smooth(r_two, extra_two, 3, 1.0)
    left = r_two - operate(solved, extra_two)
    shift_line = jnp.sum(left, axis=2, keepdims=True) / jnp.sum(1.0 + extra_two, axis=2, keepdims=True)
    return solved + shift_line


def vcycle(r_zero, extra_zero, extra_one, extra_two):
    z_zero = smooth(r_zero, extra_zero, 2, 7.0)
    r_one = restrict(r_zero - operate(z_zero, extra_zero))
    z_one = smooth(r_one, extra_one, 2, 7.0)
    r_two = restrict(r_one - operate(z_one, extra_one))
    z_two = coarse(r_two, extra_two)
    z_one = z_one + prolong(z_two)
    z_one = z_one + smooth(r_one - operate(z_one, extra_one), extra_one, 2, 7.0)
    z_zero = z_zero + prolong(z_one)
    z_zero = z_zero + smooth(r_zero - operate(z_zero, extra_zero), extra_zero, 2, 7.0)
    return z_zero


def reference(right_side, diagonal):
    extra_one = blocks(diagonal).mean(axis=(1, 3, 5))
    extra_two = blocks(extra_one).mean(axis=(1, 3, 5))
    solution_field = jnp.zeros_like(right_side)
    residual = right_side
    direction = jnp.zeros_like(right_side)
    rz_prev = jnp.float32(1.0)
    for step in range(ITERS):
        precond = vcycle(residual, diagonal, extra_one, extra_two)
        rz_now = jnp.sum(residual * precond)
        beta = 0.0 if step == 0 else rz_now / rz_prev
        direction = precond + beta * direction
        image = operate(direction, diagonal)
        alpha = rz_now / jnp.sum(direction * image)
        solution_field = solution_field + alpha * direction
        residual = residual - alpha * image
        rz_prev = rz_now
    return solution_field, residual
```

```python
import functools

import jax
import jax.numpy as jnp
from jax import lax
from jax.experimental import pallas as pl
from jax.experimental.pallas import tpu as pltpu
from jax.sharding import PartitionSpec as P

GX, GY, GZ = 4, 8, 8
BX, BY, BZ = 16, 32, 128
HX, HY, HZ = 12, 16, 64
EX, EY, EZ = BX + 2 * HX, BY + 2 * HY, BZ + 2 * HZ
MX, MY, MZ = EX // 2, EY // 2, EZ // 2
F32 = jnp.float32
HIGH = lax.Precision.HIGHEST
SPEC = P("gx", "gy", "gz")


def cheb_two(lower, upper=58.0):
    theta, delta = (upper + lower) / 2.0, (upper - lower) / 2.0
    sigma = theta / delta
    rho = 1.0 / sigma
    after = 1.0 / (2.0 * sigma - rho)
    return (1.0 + after * rho) / theta + 2.0 * after / delta, -2.0 * after / (delta * theta)


CR, CA = cheb_two(7.0)


def spread(t):
    t = t + pltpu.roll(t, 1, 0) + pltpu.roll(t, t.shape[0] - 1, 0)
    return t + pltpu.roll(t, 1, 1) + pltpu.roll(t, t.shape[1] - 1, 1)


def inside(first, dim, shape, count):
    spot = first + lax.broadcasted_iota(jnp.int32, shape, dim)
    return jnp.where((spot >= 0) & (spot < count), 1.0, 0.0).astype(F32)


def inside_one(spot, count):
    return jnp.where((spot >= 0) & (spot < count), 1.0, 0.0).astype(F32)


def places():
    return lax.axis_index("gx"), lax.axis_index("gy"), lax.axis_index("gz")


def plane_mask(level, shape, rows):
    _, gy, gz = places()
    size = 1 << level
    lanes = gz * (BZ // size) - HZ // size
    return inside(gy * (BY // size) - rows, 0, shape, GY * BY // size) * inside(
        lanes, 1, shape, GZ * BZ // size
    )


def x_mask(level, plane):
    gx = places()[0]
    size = 1 << level
    return inside_one(gx * (BX // size) - HX // size + plane, GX * BX // size)


def loop(first, last, body, unroll=1):
    def step(i, carry):
        body(i)
        return carry

    lax.fori_loop(first, last, step, 0, unroll=unroll)


def halving(rows, cols, per=2):
    a = lax.broadcasted_iota(jnp.int32, (rows, cols), 0)
    b = lax.broadcasted_iota(jnp.int32, (rows, cols), 1)
    return jnp.where(a // 2 == b, 1.0, 0.0).astype(F32)


def doubling(rows, cols):
    a = lax.broadcasted_iota(jnp.int32, (rows, cols), 0)
    b = lax.broadcasted_iota(jnp.int32, (rows, cols), 1)
    return jnp.where(b // 2 == a, 1.0, 0.0).astype(F32)


def dot(a, b):
    return jnp.dot(a, b, precision=HIGH, preferred_element_type=F32)


def assemble(dst, which, own, xlo, xhi, ylo, yhi, change):
    def part(src, base, count, lo, hi):
        def body(i):
            dst[base + i, lo:hi, :] = change(src[which, i], base + i, lo, hi)

        loop(0, count, body)

    part(own, HX, BX, HY, HY + BY)
    part(xlo, 0, HX, HY, HY + BY)
    part(xhi, HX + BX, HX, HY, HY + BY)
    part(ylo, 0, EX, 0, HY)
    part(yhi, 0, EX, HY + BY, EY)


def halve(scratch, rows_scratch, z_map):
    rows_scratch[...] = dot(scratch[...], z_map)
    count = rows_scratch.shape[0] // 2
    return rows_scratch[pl.ds(0, count, stride=2), :] + rows_scratch[pl.ds(1, count, stride=2), :]


def pre_kernel(first, own, xlo, xhi, ylo, yhi, *refs):
    d0, d1, zs, rs, z1, left1, packed, field, zfull, pairs, rows, r1, small = refs
    gx, gy, gz = places()
    mask = plane_mask(0, (EY, EZ), HY)
    z_map = halving(EZ, MZ)

    assemble(
        field, 0, own, xlo, xhi, ylo, yhi,
        lambda v, p, lo, hi: v * (mask[lo:hi] * x_mask(0, p)),
    )
    if first:
        assemble(d0, 1, own, xlo, xhi, ylo, yhi, lambda v, p, lo, hi: v + 27.0)

        def add_pair(i):
            pairs[pl.ds(pl.multiple_of(i * EY, EY), EY), :] = d0[2 * i] + d0[2 * i + 1]

        loop(0, MX, add_pair)
        d1[...] = (halve(pairs, rows, z_map) * 0.125).reshape(MX, MY, MZ)

    pairs[0:EY, :] = jnp.zeros((EY, EZ), F32)
    pairs[(MX - 1) * EY :, :] = jnp.zeros((EY, EZ), F32)

    def smooth(p):
        r = field[p]
        box = spread(field[p - 1] + r + field[p + 1])
        zfull[p] = (mask * x_mask(0, p)) * (CR * r + CA * (d0[p] * r - box))

    loop(1, EX - 1, smooth)

    def rest(p):
        z = zfull[p]
        return field[p] - d0[p] * z + spread(zfull[p - 1] + z + zfull[p + 1])

    def rest_pair(i):
        a, b = rest(2 * i), rest(2 * i + 1)
        pairs[pl.ds(pl.multiple_of(i * EY, EY), EY), :] = a + b

        @pl.when((i >= 5) & (i < 15))
        def _():
            rs[2 * i - 10] = a[8:56]
            rs[2 * i - 9] = b[8:56]

    loop(1, MX - 1, rest_pair)

    def keep(p):
        zs[p] = zfull[p + 10, 8:56, :]

    loop(0, 20, keep)

    mask1 = plane_mask(1, (MY, MZ), HY // 2)
    r1[...] = (halve(pairs, rows, z_map) * 0.5).reshape(MX, MY, MZ)

    def mask_one(p):
        r1[p] = r1[p] * (mask1 * x_mask(1, p))

    loop(0, MX, mask_one)

    def smooth_one(p):
        r = r1[p]
        box = spread(r1[p - 1] + r + r1[p + 1])
        z1[p] = (mask1 * x_mask(1, p)) * (CR * r + CA * (d1[p] * r - box))

    z1[0] = jnp.zeros((MY, MZ), F32)
    z1[MX - 1] = jnp.zeros((MY, MZ), F32)
    left1[0] = jnp.zeros((MY, MZ), F32)
    left1[MX - 1] = jnp.zeros((MY, MZ), F32)
    loop(1, MX - 1, smooth_one)

    def rest_one(p):
        z = z1[p]
        left1[p] = r1[p] - d1[p] * z + spread(z1[p - 1] + z + z1[p + 1])

    loop(1, MX - 1, rest_one)

    lane = lax.broadcasted_iota(jnp.int32, (MZ, 128), 0)
    col = lax.broadcasted_iota(jnp.int32, (MZ, 128), 1)

    def pack(src, scale):
        total = jnp.zeros((16, 128), F32)
        for k in range(4):
            s = src[6 + 2 * k, 8:24, :] + src[7 + 2 * k, 8:24, :]
            pick = (lane // 2 - 16 + 32 * k == col) & (lane >= 32) & (lane < 96)
            total = total + dot(s, jnp.where(pick, 1.0, 0.0).astype(F32))
        small[...] = total
        return (small[pl.ds(0, 8, stride=2), :] + small[pl.ds(1, 8, stride=2), :]) * scale

    tile = pack(left1, 0.5)
    if first:
        tile = jnp.concatenate([tile, pack(d1, 0.125)], axis=0)

    def copy(i):
        packed[i] = tile

    loop(0, GX * GZ, copy)


def unpack(dst, row, lo, own, hi):
    group = lax.broadcasted_iota(jnp.int32, (8, 128), 1) // 32
    for part, src in enumerate((lo, own, hi)):
        for bx in range(GX):
            for k in range(4):
                halves = []
                for h in range(2):
                    acc = None
                    for j in range(4):
                        block = src[bx * GZ + 4 * h + j, row : row + 8, :]
                        shift = (32 * (j - k)) % 128
                        if shift:
                            block = pltpu.roll(block, shift, 1)
                        acc = block if acc is None else jnp.where(group == j, block, acc)
                    halves.append(acc)
                dst[1 + 4 * bx + k, 8 * part : 8 * part + 8, :] = jnp.concatenate(halves, axis=1)


def coarse(r2, d2, s0, s1, z2, gy):
    shape = (24, 256)
    mask = inside(gy * 8 - 8, 0, shape, 64)
    lane = lax.broadcasted_iota(jnp.int32, shape, 1)

    def box(t):
        t = t + pltpu.roll(t, 1, 0) + pltpu.roll(t, 23, 0)
        return (
            t
            + jnp.where(lane == 0, 0.0, pltpu.roll(t, 1, 1))
            + jnp.where(lane == 255, 0.0, pltpu.roll(t, 255, 1))
        )

    theta, delta = 29.5, 28.5
    sigma = theta / delta
    rho = 1.0 / sigma
    rho1 = 1.0 / (2.0 * sigma - rho)
    rho2 = 1.0 / (2.0 * sigma - rho1)
    zero = jnp.zeros(shape, F32)
    for ref in (r2, s0, s1, z2):
        ref[0] = zero
        ref[17] = zero

    def scale(p):
        r2[p] = r2[p] * mask

    loop(1, 17, scale)

    def one(p):
        r = r2[p]
        step = r * (1.0 / theta)
        remain = mask * (r - d2[p] * step + box(r2[p - 1] + r + r2[p + 1]) * (1.0 / theta))
        s0[p] = remain
        s1[p] = (rho1 * rho) * step + (2.0 * rho1 / delta) * remain

    loop(1, 17, one)

    def two(p):
        step = s1[p]
        remain = mask * (s0[p] - d2[p] * step + box(s1[p - 1] + step + s1[p + 1]))
        last = (rho2 * rho1) * step + (2.0 * rho2 / delta) * remain
        z2[p] = r2[p] * (1.0 / theta) + step + last

    loop(1, 17, two)

    def three(p):
        y = z2[p]
        left = r2[p] - d2[p] * y + box(z2[p - 1] + y + z2[p + 1])
        top = jnp.sum(left, axis=1, keepdims=True)
        low = jnp.sum(d2[p] - 26.0, axis=1, keepdims=True)
        s0[p] = mask * (y + top / low)

    loop(1, 17, three)


def post_kernel(first, *refs):
    if first:
        (lo, own, hi, zs, rs, z1, left1, d0, d1, r_core,
         d2, z_core, q_core, q_ext, dots,
         r2, s0, s1, z2, wide, rows1, u, rem, zf1, rowsv, v, rem0, zf0, acc) = refs
    else:
        (lo, own, hi, zs, rs, z1, left1, d0, d1, d2,
         z_core, q_core,
         r2, s0, s1, z2, wide, rows1, u, rem, zf1, rowsv, v, rem0, zf0) = refs
    gx, gy, gz = places()
    unpack(r2, 0, lo, own, hi)
    if first:
        unpack(d2, 8, lo, own, hi)
    coarse(r2, d2, s0, s1, z2, gy)

    lane2 = lax.broadcasted_iota(jnp.int32, (16, 128), 1) + (32 * gz - 16)
    in2 = jnp.where((lane2 >= 0) & (lane2 < 256), 1.0, 0.0).astype(F32)
    shift = (256 + 16 - 32 * gz) % 256
    for i in range(10):
        p = 4 * gx - 3 + i
        spot = jnp.clip(p + 1, 0, 17)
        plane = pltpu.roll(s0[spot], shift, 1)[4:20, :128]
        wide[16 * i : 16 * i + 16, :] = plane * (in2 * inside_one(p, 16))
    up = dot(wide[...], doubling(128, 128))
    rows1[pl.ds(0, 160, stride=2), :] = up
    rows1[pl.ds(1, 160, stride=2), :] = up
    u[...] = rows1[...].reshape(10, 32, 128)

    mask1 = plane_mask(1, (MY, MZ), HY // 2)

    def remain_one(p):
        c = u[p // 2]
        total = u[(p - 1) // 2] + c + u[(p + 1) // 2]
        rem[p] = (mask1 * x_mask(1, p)) * (left1[p] - d1[p] * c + spread(total))

    loop(3, 17, remain_one)

    def final_one(p):
        r = rem[p]
        box = spread(rem[p - 1] + r + rem[p + 1])
        f = z1[p] + u[p // 2] + (mask1 * x_mask(1, p)) * (CR * r + CA * (d1[p] * r - box))
        zf1[pl.ds(pl.multiple_of((p - 4) * 24, 8), 24), :] = f[4:28]

    loop(4, 16, final_one)

    v_count = 12 * 24
    rowsv[pl.ds(0, v_count, stride=2), :] = zf1[...]
    rowsv[pl.ds(1, v_count, stride=2), :] = zf1[...]
    v[...] = dot(rowsv[...], doubling(128, 256)).reshape(12, 48, 256)

    mask0 = plane_mask(0, (48, EZ), HY - 8)

    def remain(i):
        p = i + 10
        c = v[p // 2 - 4]
        total = v[(p - 1) // 2 - 4] + c + v[(p + 1) // 2 - 4]
        rem0[i] = (mask0 * x_mask(0, p)) * (rs[i] - d0[p, 8:56, :] * c + spread(total))

    loop(0, 20, remain)

    def final(i):
        p = i + 10
        r = rem0[i]
        box = spread(rem0[i - 1] + r + rem0[i + 1])
        zf0[i] = zs[i] + v[p // 2 - 4] + (mask0 * x_mask(0, p)) * (
            CR * r + CA * (d0[p, 8:56, :] * r - box)
        )

    loop(1, 19, final)

    if first:
        acc[...] = jnp.zeros((2, BY, BZ), F32)

    def apply(i):
        c = zf0[i + 2]
        q = d0[i + HX, 8:56, :] * c - spread(zf0[i + 1] + c + zf0[i + 3])
        qc = pltpu.roll(q, EZ - HZ, 1)[8:40, :BZ]
        zc = pltpu.roll(c, EZ - HZ, 1)[8:40, :BZ]
        z_core[i] = zc
        q_core[i] = qc
        if first:
            q_ext[0, i] = q[8:40]
            acc[0] += r_core[i] * zc
            acc[1] += zc * qc

    loop(0, BX, apply)
    if first:
        store_dots(dots, [acc[0], acc[1]])


def store_dots(dots, parts):
    rows = [jnp.sum(part, axis=0, keepdims=True) for part in parts]
    rows.append(jnp.zeros((8 - len(parts), BZ), F32))
    dots[...] = jnp.concatenate(rows, axis=0)


def pick(tile, row):
    return jnp.sum(tile[row : row + 1, :], axis=1, keepdims=True)


def dots_kernel(r, z, q, p, w, sums, dots, acc):
    tile = sums[...]
    alpha = pick(tile, 0) / pick(tile, 1)
    acc[...] = jnp.zeros((3, BY, BZ), F32)

    def body(i):
        qi = q[i]
        z2 = z[i] - alpha * p[i]
        acc[0] += (r[i] - alpha * qi) * z2
        acc[1] += z2 * (qi - alpha * w[i])
        acc[2] += z2 * qi

    loop(0, BX, body)
    store_dots(dots, [acc[0], acc[1], acc[2]])


def end_kernel(r, z, q, p, w, sums, more, solution_field, residual):
    tile, last = sums[...], more[...]
    rz, curve = pick(tile, 0), pick(tile, 1)
    alpha = rz / curve
    rz2 = pick(last, 0)
    beta = rz2 / rz
    alpha2 = rz2 / (pick(last, 1) + 2.0 * beta * pick(last, 2) + beta * beta * curve)

    def body(i):
        zi, qi = z[i], q[i]
        solution_field[i] = alpha * zi + alpha2 * ((zi - alpha * p[i]) + beta * zi)
        residual[i] = (r[i] - alpha * qi) - alpha2 * ((qi - alpha * w[i]) + beta * qi)

    loop(0, BX, body)


def shape(*dims):
    return jax.ShapeDtypeStruct(dims, F32)


def call(kernel, outs, scratch, *args):
    whole = pl.BlockSpec(memory_space=pltpu.VMEM)
    return pl.pallas_call(
        kernel,
        out_shape=outs,
        in_specs=[whole] * len(args),
        out_specs=jax.tree.map(lambda _: whole, outs),
        scratch_shapes=[pltpu.VMEM(s, F32) for s in scratch],
        compiler_params=pltpu.CompilerParams(vmem_limit_bytes=48 * 1024 * 1024),
    )(*args)


def shift(value, axis, count, by):
    return lax.ppermute(value, axis, [(i, (i + by) % count) for i in range(count)])


def exchange_xy(own):
    xlo = shift(own[:, BX - HX :], "gx", GX, 1)
    xhi = shift(own[:, :HX], "gx", GX, -1)
    tall = jnp.concatenate([xlo, own, xhi], axis=1)
    ylo = shift(tall[:, :, BY - HY :], "gy", GY, 1)
    yhi = shift(tall[:, :, :HY], "gy", GY, -1)
    return own, xlo, xhi, ylo, yhi


def all_sum(tile):
    wide = jnp.broadcast_to(tile, (GY * GZ, 8, 128))
    part = lax.all_to_all(wide, ("gy", "gz"), 0, 0).sum(axis=0)
    return part + shift(part, "gx", GX, 1) + shift(part, "gx", GX, 2) + shift(part, "gx", GX, 3)


def spread_coarse(packed):
    own = lax.all_to_all(packed, ("gx", "gz"), 0, 0)
    return shift(own, "gy", GY, 1), own, shift(own, "gy", GY, -1)


def pre_call(pieces, given):
    first = given is None
    kept = (shape(20, 48, EZ), shape(20, 48, EZ), shape(MX, MY, MZ), shape(MX, MY, MZ),
            shape(GX * GZ, 16 if first else 8, 128))
    scratch = [(EX, EY, EZ), (EX, EY, EZ), (MX * EY, EZ), (MX * EY, MZ), (MX, MY, MZ), (16, 128)]
    kernel = functools.partial(pre_kernel, first)
    if first:
        return call(kernel, (shape(EX, EY, EZ), shape(MX, MY, MZ)) + kept, scratch, *pieces)
    return call(kernel, kept, scratch, *pieces, *given)


def post_call(parts, kept, d0, d1, r_core=None, d2=None):
    first = d2 is None
    scratch = [(18, 24, 256)] * 4 + [
        (160, 128), (320, 128), (10, 32, 128), (MX, MY, MZ), (288, 128),
        (576, 128), (12, 48, EZ), (20, 48, EZ), (20, 48, EZ),
    ]
    core = shape(BX, BY, BZ)
    kernel = functools.partial(post_kernel, first)
    if first:
        outs = (shape(18, 24, 256), core, core, shape(1, BX, BY, EZ), shape(8, 128))
        return call(kernel, outs, scratch + [(2, BY, BZ)], *parts, *kept, d0, d1, r_core)
    return call(kernel, (core, core), scratch, *parts, *kept, d0, d1, d2)


def local(right_side, diagonal):
    both = jnp.stack([right_side, diagonal])
    left = shift(both[..., BZ - HZ :], "gz", GZ, 1)
    right = shift(both[..., :HZ], "gz", GZ, -1)
    both = jnp.concatenate([left, both, right], axis=3)
    d0, d1, *kept = pre_call(exchange_xy(both), None)
    d2, z, q, q_ext, dots = post_call(
        spread_coarse(kept[-1]), kept[:-1], d0, d1, r_core=right_side
    )
    sums = all_sum(dots)
    kept = pre_call(exchange_xy(q_ext), (d0, d1))
    p, w = post_call(spread_coarse(kept[-1]), kept[:-1], d0, d1, d2=d2)
    fields = (right_side, z, q, p, w)
    more = call(dots_kernel, shape(8, 128), [(3, BY, BZ)], *fields, sums)
    core = shape(BX, BY, BZ)
    return call(end_kernel, (core, core), [], *fields, sums, all_sum(more))


def solution(mesh):
    return jax.shard_map(
        local, mesh=mesh, in_specs=(SPEC, SPEC), out_specs=(SPEC, SPEC), check_vma=False
    )
```

```python
import functools

import jax
import jax.numpy as jnp
from jax import lax
from jax.experimental import pallas as pl
from jax.experimental.pallas import tpu as pltpu
from jax.sharding import PartitionSpec as P

GX, GY, GZ = 4, 8, 8
BX, BY, BZ = 16, 32, 128
HX, HY, HZ = 12, 16, 64
EX, EY, EZ = BX + 2 * HX, BY + 2 * HY, BZ + 2 * HZ
MX, MY, MZ = EX // 2, EY // 2, EZ // 2
F32 = jnp.float32
SPEC = P("gx", "gy", "gz")


def cheb_two(lower, upper=58.0):
    theta, delta = (upper + lower) / 2.0, (upper - lower) / 2.0
    sigma = theta / delta
    rho = 1.0 / sigma
    after = 1.0 / (2.0 * sigma - rho)
    return (1.0 + after * rho) / theta + 2.0 * after / delta, -2.0 * after / (delta * theta)


CR, CA = cheb_two(7.0)


def spread(t):
    t = t + pltpu.roll(t, 1, 0) + pltpu.roll(t, t.shape[0] - 1, 0)
    return t + pltpu.roll(t, 1, 1) + pltpu.roll(t, t.shape[1] - 1, 1)


def inside(first, dim, shape, count):
    spot = first + lax.broadcasted_iota(jnp.int32, shape, dim)
    return jnp.where((spot >= 0) & (spot < count), 1.0, 0.0).astype(F32)


def inside_one(spot, count):
    return jnp.where((spot >= 0) & (spot < count), 1.0, 0.0).astype(F32)


def places():
    return lax.axis_index("gx"), lax.axis_index("gy"), lax.axis_index("gz")


def plane_mask(level, shape, rows):
    _, gy, gz = places()
    size = 1 << level
    lanes = gz * (BZ // size) - HZ // size
    return inside(gy * (BY // size) - rows, 0, shape, GY * BY // size) * inside(
        lanes, 1, shape, GZ * BZ // size
    )


def x_mask(level, plane):
    gx = places()[0]
    size = 1 << level
    return inside_one(gx * (BX // size) - HX // size + plane, GX * BX // size)


def loop(first, last, body):
    for i in range(first, last):
        body(i)


def halving(rows, cols, per=2):
    a = lax.broadcasted_iota(jnp.int32, (rows, cols), 0)
    b = lax.broadcasted_iota(jnp.int32, (rows, cols), 1)
    return jnp.where(a // 2 == b, 1.0, 0.0).astype(F32)


def doubling(rows, cols):
    a = lax.broadcasted_iota(jnp.int32, (rows, cols), 0)
    b = lax.broadcasted_iota(jnp.int32, (rows, cols), 1)
    return jnp.where(b // 2 == a, 1.0, 0.0).astype(F32)


def dot(a, b):
    b = b.astype(jnp.bfloat16)
    hi = a.astype(jnp.bfloat16)
    a = a - hi.astype(F32)
    mid = a.astype(jnp.bfloat16)
    lo = (a - mid.astype(F32)).astype(jnp.bfloat16)
    one = functools.partial(jnp.dot, preferred_element_type=F32)
    return one(hi, b) + one(mid, b) + one(lo, b)


def join(center, left, right, first, last):
    lane = lax.broadcasted_iota(jnp.int32, center.shape, 1)
    turned = pltpu.roll(center, HZ, 1)
    low = jnp.where(lane >= HZ, turned, jnp.where(lane >= first, left, 0.0))
    high = jnp.where(lane < HZ, turned, jnp.where(lane < last, right, 0.0))
    return low, high


def half_tile(src, base, plane, upper):
    tile = src[base + plane // 2]
    return tile if plane % 2 == upper else pltpu.roll(tile, 4, 0)


def assemble(dst, parts, change):
    for p in range(EX):
        for lo, hi, (center, left, right, first, last) in parts(p):
            low, high = join(center, left, right, first, last)
            dst[p, lo:hi, 0:128] = change(low, p, lo, hi, 0)
            dst[p, lo:hi, 128:256] = change(high, p, lo, hi, 128)


def turn(tile, by):
    by = by % 128
    return pltpu.roll(tile, by, 1) if by else tile


def x_plane(own, xlo, xhi, p):
    if p < HX:
        return xlo(p)
    return own(p - HX) if p < HX + BX else xhi(p - HX - BX)


def first_parts(a, own, xlo, xhi, zl, zr, ylo, yhi):
    base = a * 90

    def parts(p):
        g, k = p // 4, p % 4
        sides = lambda l, r: (turn(l, 32 - 32 * k), turn(r, 64 - 32 * k), 32, 96)
        center = x_plane(
            lambda i: own[i], lambda i: xlo[a, i], lambda i: xhi[a, i], p
        )
        whole = lambda y: (y[base + p], *sides(y[base + 40 + g], y[base + 50 + g]))
        half = lambda y, upper: (
            half_tile(y, base + 60, p, upper),
            *sides(
                half_tile(y, base + 60, 40 + g, upper), half_tile(y, base + 60, 50 + g, upper)
            ),
        )
        return [
            (0, 8, half(ylo, 1)),
            (8, 16, whole(ylo)),
            (16, 48, (center, *sides(zl[a, g], zr[a, g]))),
            (48, 56, whole(yhi)),
            (56, 64, half(yhi, 0)),
        ]

    return parts


def later_parts(own, halo, xlo, xhi, ylo, yhi):
    def parts(p):
        g, k = p // 4, p % 4
        sides = lambda h: (turn(h, 48 - 32 * k),) * 2 + (48, 80)
        center = x_plane(lambda i: own[i], lambda i: xlo[i], lambda i: xhi[i], p)
        side = x_plane(
            lambda i: halo[i // 4], lambda i: xlo[12 + i // 4], lambda i: xhi[12 + i // 4], p
        )
        whole = lambda y: (y[p], *sides(y[40 + g]))
        half = lambda y, upper: (
            half_tile(y, 50, p, upper), *sides(half_tile(y, 50, 40 + g, upper))
        )
        return [
            (0, 8, half(ylo, 1)),
            (8, 16, whole(ylo)),
            (16, 48, (center, *sides(side))),
            (48, 56, whole(yhi)),
            (56, 64, half(yhi, 0)),
        ]

    return parts


def z_pack_kernel(right_side, diagonal, xlo, xhi, down, up):
    group = lax.broadcasted_iota(jnp.int32, (BY, BZ), 1) // 32
    for a, own in enumerate((right_side, diagonal)):
        for g in range(EX // 4):
            low = high = None
            for k in range(4):
                src = x_plane(
                    lambda i: own[i], lambda i: xlo[a, i], lambda i: xhi[a, i], 4 * g + k
                )
                first, last = turn(src, 32 * k), turn(src, 32 * k - 96)
                low = first if k == 0 else jnp.where(group == k, first, low)
                high = last if k == 0 else jnp.where(group == k, last, high)
            down[a, g] = low
            up[a, g] = high


def y_rows(planes, base, down, up):
    count = len(planes)
    for m, plane in enumerate(planes):
        down[base + m] = plane(0, 8)
        up[base + m] = plane(24, 32)
    for m in range(0, count, 2):
        one, two = planes[m], planes[m + 1]
        at = base + count + m // 2
        down[at] = jnp.concatenate([one(8, 12), two(8, 12)], axis=0)
        up[at] = jnp.concatenate([one(20, 24), two(20, 24)], axis=0)


def y_pack_kernel(right_side, diagonal, xlo, xhi, zl, zr, down, up):
    def rows(ref, *index):
        return lambda lo, hi: ref[(*index, slice(lo, hi))]

    for a, own in enumerate((right_side, diagonal)):
        planes = [
            x_plane(
                lambda i: rows(own, i), lambda i: rows(xlo, a, i), lambda i: rows(xhi, a, i), p
            )
            for p in range(EX)
        ]
        planes += [rows(zl, a, g) for g in range(10)] + [rows(zr, a, g) for g in range(10)]
        y_rows(planes, 90 * a, down, up)


def y_pack_later_kernel(own, halo, xlo, xhi, dots, down, up):
    def rows(ref, index):
        return lambda lo, hi: ref[index, lo:hi]

    planes = [
        x_plane(lambda i: rows(own, i), lambda i: rows(xlo, i), lambda i: rows(xhi, i), p)
        for p in range(EX)
    ]
    planes += [
        x_plane(
            lambda i: rows(halo, i // 4),
            lambda i: rows(xlo, 12 + i // 4),
            lambda i: rows(xhi, 12 + i // 4),
            4 * g,
        )
        for g in range(10)
    ]
    y_rows(planes, 0, down, up)
    down[75] = dots[...]
    up[75] = dots[...]


def halve(scratch, rows_scratch, z_map):
    rows_scratch[...] = dot(scratch[...], z_map)
    count = rows_scratch.shape[0] // 2
    return rows_scratch[pl.ds(0, count, stride=2), :] + rows_scratch[pl.ds(1, count, stride=2), :]


def pre_kernel(first, *refs):
    if first:
        right_side, diagonal, xlo, xhi, zl, zr, ylo, yhi = refs[:8]
        refs = refs[8:]
        r_parts = first_parts(0, right_side, xlo, xhi, zl, zr, ylo, yhi)
        d_parts = first_parts(1, diagonal, xlo, xhi, zl, zr, ylo, yhi)
    else:
        own, halo, xlo, xhi, ylo, yhi, dots = refs[:7]
        refs = refs[7:]
        r_parts = later_parts(own, halo, xlo, xhi, ylo, yhi)
    d0, d1, zs, rs, z1, left1, packed, field, zfull, pairs, rows, r1, small = refs
    mask = plane_mask(0, (EY, EZ), HY)
    z_map = halving(EZ, MZ)

    assemble(
        field, r_parts,
        lambda v, p, lo, hi, at: v * (mask[lo:hi, at : at + 128] * x_mask(0, p)),
    )
    if first:
        assemble(d0, d_parts, lambda v, p, lo, hi, at: v + 27.0)

        def add_pair(i):
            pairs[i * EY : (i + 1) * EY, :] = d0[2 * i] + d0[2 * i + 1]

        loop(0, MX, add_pair)
        d1[...] = (halve(pairs, rows, z_map) * 0.125).reshape(MX, MY, MZ)

    pairs[0:EY, :] = jnp.zeros((EY, EZ), F32)
    pairs[(MX - 1) * EY :, :] = jnp.zeros((EY, EZ), F32)

    def smooth(p):
        r = field[p]
        box = spread(field[p - 1] + r + field[p + 1])
        zfull[p] = (mask * x_mask(0, p)) * (CR * r + CA * (d0[p] * r - box))

    loop(1, EX - 1, smooth)

    def rest(p):
        z = zfull[p]
        return field[p] - d0[p] * z + spread(zfull[p - 1] + z + zfull[p + 1])

    def rest_pair(i):
        a, b = rest(2 * i), rest(2 * i + 1)
        pairs[i * EY : (i + 1) * EY, :] = a + b

        if 5 <= i < 15:
            rs[2 * i - 10] = a[8:56]
            rs[2 * i - 9] = b[8:56]

    loop(1, MX - 1, rest_pair)

    def keep(p):
        zs[p] = zfull[p + 10, 8:56, :]

    loop(0, 20, keep)

    mask1 = plane_mask(1, (MY, MZ), HY // 2)
    r1[...] = (halve(pairs, rows, z_map) * 0.5).reshape(MX, MY, MZ)

    def mask_one(p):
        r1[p] = r1[p] * (mask1 * x_mask(1, p))

    loop(0, MX, mask_one)

    def smooth_one(p):
        r = r1[p]
        box = spread(r1[p - 1] + r + r1[p + 1])
        z1[p] = (mask1 * x_mask(1, p)) * (CR * r + CA * (d1[p] * r - box))

    z1[0] = jnp.zeros((MY, MZ), F32)
    z1[MX - 1] = jnp.zeros((MY, MZ), F32)
    left1[0] = jnp.zeros((MY, MZ), F32)
    left1[MX - 1] = jnp.zeros((MY, MZ), F32)
    loop(1, MX - 1, smooth_one)

    def rest_one(p):
        z = z1[p]
        left1[p] = r1[p] - d1[p] * z + spread(z1[p - 1] + z + z1[p + 1])

    loop(1, MX - 1, rest_one)

    lane = lax.broadcasted_iota(jnp.int32, (MZ, 128), 0)
    col = lax.broadcasted_iota(jnp.int32, (MZ, 128), 1)

    def pack(src, scale):
        total = jnp.zeros((16, 128), F32)
        for k in range(4):
            s = src[6 + 2 * k, 8:24, :] + src[7 + 2 * k, 8:24, :]
            pick = (lane // 2 - 16 + 32 * k == col) & (lane >= 32) & (lane < 96)
            total = total + dot(s, jnp.where(pick, 1.0, 0.0).astype(F32))
        small[...] = total
        return (small[pl.ds(0, 8, stride=2), :] + small[pl.ds(1, 8, stride=2), :]) * scale

    tile = pack(left1, 0.5)
    if first:
        other = pack(d1, 0.125)
    else:
        three = ylo[75] + dots[...] + yhi[75]
        other = three + pltpu.roll(dots[...] + yhi[75], 2, 0)
    tile = jnp.concatenate([tile, other], axis=0)

    def copy(i):
        packed[i] = tile

    loop(0, GX * GZ, copy)


def unpack(dst, row, lo, own, hi):
    group = lax.broadcasted_iota(jnp.int32, (8, 128), 1) // 32
    for part, src in enumerate((lo, own, hi)):
        for bx in range(GX):
            for k in range(4):
                halves = []
                for h in range(2):
                    acc = None
                    for j in range(4):
                        block = src[bx * GZ + 4 * h + j, row : row + 8, :]
                        shift = (32 * (j - k)) % 128
                        if shift:
                            block = pltpu.roll(block, shift, 1)
                        acc = block if acc is None else jnp.where(group == j, block, acc)
                    halves.append(acc)
                dst[1 + 4 * bx + k, 8 * part : 8 * part + 8, :] = jnp.concatenate(halves, axis=1)


def coarse(r2, d2, s0, s1, z2, gy):
    shape = (24, 256)
    mask = inside(gy * 8 - 8, 0, shape, 64)
    lane = lax.broadcasted_iota(jnp.int32, shape, 1)

    def box(t):
        t = t + pltpu.roll(t, 1, 0) + pltpu.roll(t, 23, 0)
        return (
            t
            + jnp.where(lane == 0, 0.0, pltpu.roll(t, 1, 1))
            + jnp.where(lane == 255, 0.0, pltpu.roll(t, 255, 1))
        )

    theta, delta = 29.5, 28.5
    sigma = theta / delta
    rho = 1.0 / sigma
    rho1 = 1.0 / (2.0 * sigma - rho)
    rho2 = 1.0 / (2.0 * sigma - rho1)
    zero = jnp.zeros(shape, F32)
    for ref in (r2, s0, s1, z2):
        ref[0] = zero
        ref[17] = zero

    def scale(p):
        r2[p] = r2[p] * mask

    loop(1, 17, scale)

    def one(p):
        r = r2[p]
        step = r * (1.0 / theta)
        remain = mask * (r - d2[p] * step + box(r2[p - 1] + r + r2[p + 1]) * (1.0 / theta))
        s0[p] = remain
        s1[p] = (rho1 * rho) * step + (2.0 * rho1 / delta) * remain

    loop(1, 17, one)

    def two(p):
        step = s1[p]
        remain = mask * (s0[p] - d2[p] * step + box(s1[p - 1] + step + s1[p + 1]))
        last = (rho2 * rho1) * step + (2.0 * rho2 / delta) * remain
        z2[p] = r2[p] * (1.0 / theta) + step + last

    loop(1, 17, two)

    def three(p):
        y = z2[p]
        left = r2[p] - d2[p] * y + box(z2[p - 1] + y + z2[p + 1])
        top = jnp.sum(left, axis=1, keepdims=True)
        low = jnp.sum(d2[p] - 26.0, axis=1, keepdims=True)
        s0[p] = mask * (y + top / low)

    loop(1, 17, three)


def post_kernel(first, *refs):
    if first:
        (lo, own, hi, zs, rs, z1, left1, d0, d1, r_core,
         d2, z_core, q_core, q_down, q_up, q_halo, dots,
         r2, s0, s1, z2, wide, rows1, u, rem, zf1, rowsv, v, rem0, zf0, acc) = refs
    else:
        (lo, own, hi, zs, rs, z1, left1, d0, d1, d2,
         z_core, q_core,
         r2, s0, s1, z2, wide, rows1, u, rem, zf1, rowsv, v, rem0, zf0) = refs
    gx, gy, gz = places()
    unpack(r2, 0, lo, own, hi)
    if first:
        unpack(d2, 8, lo, own, hi)
    coarse(r2, d2, s0, s1, z2, gy)

    lane2 = lax.broadcasted_iota(jnp.int32, (16, 128), 1) + (32 * gz - 16)
    in2 = jnp.where((lane2 >= 0) & (lane2 < 256), 1.0, 0.0).astype(F32)
    shift = (256 + 16 - 32 * gz) % 256
    for i in range(10):
        p = 4 * gx - 3 + i
        spot = jnp.clip(p + 1, 0, 17)
        plane = pltpu.roll(s0[spot], shift, 1)[4:20, :128]
        wide[16 * i : 16 * i + 16, :] = plane * (in2 * inside_one(p, 16))
    up = dot(wide[...], doubling(128, 128))
    rows1[pl.ds(0, 160, stride=2), :] = up
    rows1[pl.ds(1, 160, stride=2), :] = up
    u[...] = rows1[...].reshape(10, 32, 128)

    mask1 = plane_mask(1, (MY, MZ), HY // 2)

    def remain_one(p):
        c = u[p // 2]
        total = u[(p - 1) // 2] + c + u[(p + 1) // 2]
        rem[p] = (mask1 * x_mask(1, p)) * (left1[p] - d1[p] * c + spread(total))

    loop(3, 17, remain_one)

    def final_one(p):
        r = rem[p]
        box = spread(rem[p - 1] + r + rem[p + 1])
        f = z1[p] + u[p // 2] + (mask1 * x_mask(1, p)) * (CR * r + CA * (d1[p] * r - box))
        zf1[(p - 4) * 24 : (p - 3) * 24, :] = f[4:28]

    loop(4, 16, final_one)

    v_count = 12 * 24
    rowsv[pl.ds(0, v_count, stride=2), :] = zf1[...]
    rowsv[pl.ds(1, v_count, stride=2), :] = zf1[...]
    v[...] = dot(rowsv[...], doubling(128, 256)).reshape(12, 48, 256)

    mask0 = plane_mask(0, (48, EZ), HY - 8)

    def remain(i):
        p = i + 10
        c = v[p // 2 - 4]
        total = v[(p - 1) // 2 - 4] + c + v[(p + 1) // 2 - 4]
        rem0[i] = (mask0 * x_mask(0, p)) * (rs[i] - d0[p, 8:56, :] * c + spread(total))

    loop(0, 20, remain)

    def final(i):
        p = i + 10
        r = rem0[i]
        box = spread(rem0[i - 1] + r + rem0[i + 1])
        zf0[i] = zs[i] + v[p // 2 - 4] + (mask0 * x_mask(0, p)) * (
            CR * r + CA * (d0[p, 8:56, :] * r - box)
        )

    loop(1, 19, final)

    if first:
        acc[...] = jnp.zeros((2, BY, BZ), F32)

    lane = lax.broadcasted_iota(jnp.int32, (BY, BZ), 1)

    def apply(i):
        c = zf0[i + 2]
        q = d0[i + HX, 8:56, :] * c - spread(zf0[i + 1] + c + zf0[i + 3])
        qc = pltpu.roll(q, EZ - HZ, 1)[8:40, :BZ]
        zc = pltpu.roll(c, EZ - HZ, 1)[8:40, :BZ]
        z_core[i] = zc
        q_core[i] = qc
        if first:
            if i < 12:
                q_down[i] = qc
            if i >= 4:
                q_up[i - 4] = qc
            edge = jnp.where(lane < HZ, q[8:40, :128], q[8:40, 128:])
            edge = turn(edge, 32 * (i % 4) - 48)
            halo = edge if i % 4 == 0 else jnp.where(lane // 32 == i % 4, edge, q_halo[i // 4])
            q_halo[i // 4] = halo
            if i % 4 == 3 and i < 12:
                q_down[12 + i // 4] = halo
            if i % 4 == 3 and i >= 4:
                q_up[11 + i // 4] = halo
            acc[0] += r_core[i] * zc
            acc[1] += zc * qc

    loop(0, BX, apply)
    if first:
        store_dots(dots, [acc[0], acc[1]])


def store_dots(dots, parts):
    rows = [jnp.sum(part, axis=0, keepdims=True) for part in parts]
    rows.append(jnp.zeros((8 - len(parts), BZ), F32))
    dots[...] = jnp.concatenate(rows, axis=0)


def pick(tile, row):
    return jnp.sum(tile[row : row + 1, :], axis=1, keepdims=True)


def first_sums(here, after, before):
    h, a, b = here[...], after[...], before[...]
    return pick(h, 0) + pick(a, 0) + pick(b, 2), pick(h, 1) + pick(a, 1) + pick(b, 3)


def dots_kernel(r, z, q, p, w, here, after, before, dots, acc):
    rz, curve = first_sums(here, after, before)
    alpha = rz / curve
    acc[...] = jnp.zeros((3, BY, BZ), F32)

    def body(i):
        qi = q[i]
        z2 = z[i] - alpha * p[i]
        acc[0] += (r[i] - alpha * qi) * z2
        acc[1] += z2 * (qi - alpha * w[i])
        acc[2] += z2 * qi

    loop(0, BX, body)
    lane = lax.broadcasted_iota(jnp.int32, (1, 128), 1)
    row = jnp.zeros((1, 128), F32)
    for i in range(3):
        total = jnp.sum(jnp.sum(acc[i], axis=0, keepdims=True), axis=1, keepdims=True)
        row = jnp.where(lane == i, total, row)
    dots[...] = jnp.broadcast_to(row[None], (GY * GZ, 1, 128))


def end_kernel(r, z, q, p, w, here, after, before, m0, m1, m2, m3, solution_field, residual):
    rz, curve = first_sums(here, after, before)
    alpha = rz / curve
    last = jnp.sum(m0[...] + m1[...] + m2[...] + m3[...], axis=0)
    lane = lax.broadcasted_iota(jnp.int32, (1, 128), 1)
    at = lambda i: jnp.sum(jnp.where(lane == i, last, 0.0), axis=1, keepdims=True)
    rz2 = at(0)
    beta = rz2 / rz
    alpha2 = rz2 / (at(1) + 2.0 * beta * at(2) + beta * beta * curve)

    def body(i):
        zi, qi = z[i], q[i]
        solution_field[i] = alpha * zi + alpha2 * ((zi - alpha * p[i]) + beta * zi)
        residual[i] = (r[i] - alpha * qi) - alpha2 * ((qi - alpha * w[i]) + beta * qi)

    loop(0, BX, body)


def shape(*dims):
    return jax.ShapeDtypeStruct(dims, F32)


def call(kernel, outs, scratch, *args):
    whole = pl.BlockSpec(memory_space=pltpu.VMEM)
    return pl.pallas_call(
        kernel,
        out_shape=outs,
        in_specs=[whole] * len(args),
        out_specs=jax.tree.map(lambda _: whole, outs),
        scratch_shapes=[pltpu.VMEM(s, F32) for s in scratch],
        compiler_params=pltpu.CompilerParams(vmem_limit_bytes=24 * 1024 * 1024),
    )(*args)


def shift(value, axis, count, by):
    return lax.ppermute(value, axis, [(i, (i + by) % count) for i in range(count)])


def spread_coarse(packed):
    own = lax.all_to_all(packed, ("gx", "gz"), 0, 0)
    return shift(own, "gy", GY, 1), own, shift(own, "gy", GY, -1)


def pre_call(first, *args):
    kept = (shape(20, 48, EZ), shape(20, 48, EZ), shape(MX, MY, MZ), shape(MX, MY, MZ),
            shape(GX * GZ, 16, 128))
    scratch = [(EX, EY, EZ), (EX, EY, EZ), (MX * EY, EZ), (MX * EY, MZ), (MX, MY, MZ), (16, 128)]
    kernel = functools.partial(pre_kernel, first)
    if first:
        kept = (shape(EX, EY, EZ), shape(MX, MY, MZ)) + kept
    return call(kernel, kept, scratch, *args)


def post_call(parts, kept, d0, d1, r_core=None, d2=None):
    first = d2 is None
    scratch = [(18, 24, 256)] * 4 + [
        (160, 128), (320, 128), (10, 32, 128), (MX, MY, MZ), (288, 128),
        (576, 128), (12, 48, EZ), (20, 48, EZ), (20, 48, EZ),
    ]
    core = shape(BX, BY, BZ)
    kernel = functools.partial(post_kernel, first)
    if first:
        slab = shape(15, BY, BZ)
        outs = (shape(18, 24, 256), core, core, slab, slab, shape(4, BY, BZ), shape(8, 128))
        return call(kernel, outs, scratch + [(2, BY, BZ)], *parts, *kept, d0, d1, r_core)
    return call(kernel, (core, core), scratch, *parts, *kept, d0, d1, d2)


def first_exchange(right_side, diagonal):
    def slab(lo, hi):
        return jnp.stack([right_side[lo:hi], diagonal[lo:hi]])

    xlo = shift(slab(BX - HX, BX), "gx", GX, 1)
    xhi = shift(slab(0, HX), "gx", GX, -1)
    edge = shape(2, EX // 4, BY, BZ)
    down, up = call(z_pack_kernel, (edge, edge), [], right_side, diagonal, xlo, xhi)
    zl = shift(up, "gz", GZ, 1)
    zr = shift(down, "gz", GZ, -1)
    edge = shape(180, 8, BZ)
    pieces = (right_side, diagonal, xlo, xhi, zl, zr)
    down, up = call(y_pack_kernel, (edge, edge), [], *pieces)
    return *pieces, shift(up, "gy", GY, 1), shift(down, "gy", GY, -1)


def later_exchange(q, q_down, q_up, q_halo, dots):
    xlo = shift(q_up, "gx", GX, 1)
    xhi = shift(q_down, "gx", GX, -1)
    edge = shape(76, 8, BZ)
    down, up = call(y_pack_later_kernel, (edge, edge), [], q, q_halo, xlo, xhi, dots)
    return q, q_halo, xlo, xhi, shift(up, "gy", GY, 1), shift(down, "gy", GY, -1), dots


def local(right_side, diagonal):
    d0, d1, *kept = pre_call(True, *first_exchange(right_side, diagonal))
    d2, z, q, *edges = post_call(
        spread_coarse(kept[-1]), kept[:-1], d0, d1, r_core=right_side
    )
    kept = pre_call(False, *later_exchange(q, *edges), d0, d1)
    parts = spread_coarse(kept[-1])
    here = jnp.sum(parts[1][:, 8:], axis=0)
    sums = (here, shift(here, "gy", GY, -3), shift(here, "gy", GY, 3))
    p, w = post_call(parts, kept[:-1], d0, d1, d2=d2)
    fields = (right_side, z, q, p, w)
    more = call(dots_kernel, shape(GY * GZ, 1, 128), [(3, BY, BZ)], *fields, *sums)
    more = lax.all_to_all(more, ("gy", "gz"), 0, 0)
    others = [shift(more, "gx", GX, i) for i in (1, 2, 3)]
    core = shape(BX, BY, BZ)
    return call(end_kernel, (core, core), [], *fields, *sums, more, *others)


def solution(mesh):
    return jax.shard_map(
        local, mesh=mesh, in_specs=(SPEC, SPEC), out_specs=(SPEC, SPEC), check_vma=False
    )
```

```python
import functools

import jax
import jax.numpy as jnp
from jax import lax
from jax.experimental import pallas as pl
from jax.experimental.pallas import tpu as pltpu
from jax.sharding import PartitionSpec as P

GX, GY, GZ = 4, 8, 8
BX, BY, BZ = 16, 32, 128
HX, HY = 12, 12
EX, EY, EZ = BX + 2 * HX, BY + 2 * HY, 2 * BZ
MX, MR, MY, MZ = EX // 2, EY // 2, 32, BZ
PY = BY + 8
F32 = jnp.float32
SPEC = P("gx", "gy", "gz")


def cheb_two(lower, upper=58.0):
    theta, delta = (upper + lower) / 2.0, (upper - lower) / 2.0
    sigma = theta / delta
    rho = 1.0 / sigma
    after = 1.0 / (2.0 * sigma - rho)
    return (1.0 + after * rho) / theta + 2.0 * after / delta, -2.0 * after / (delta * theta)


CR, CA = cheb_two(7.0)


def spread(t):
    t = t + pltpu.roll(t, 1, 0) + pltpu.roll(t, t.shape[0] - 1, 0)
    return t + pltpu.roll(t, 1, 1) + pltpu.roll(t, t.shape[1] - 1, 1)


def flag(condition):
    return jnp.where(condition, 1.0, 0.0).astype(F32)


def places():
    return lax.axis_index("gx"), lax.axis_index("gy"), lax.axis_index("gz")


def plane_mask(level, shape, row):
    _, gy, gz = places()
    size = 1 << level
    y = lax.broadcasted_iota(jnp.int32, shape, 0) + (gy * (BY // size) + row)
    lane = lax.broadcasted_iota(jnp.int32, shape, 1)
    z = jnp.where(lane < 3 * shape[1] // 4, lane, lane - shape[1]) + gz * (BZ // size)
    return flag((y >= 0) & (y < GY * BY // size) & (z >= 0) & (z < GZ * BZ // size))


def x_masks(mask, level, scale=1.0):
    gx = places()[0]
    first, last = HX >> level, (HX + BX) >> level
    low, high = flag(gx > 0) * scale, flag(gx < GX - 1) * scale
    low, mid, high = mask * low, mask * scale, mask * high
    return lambda p: low if p < first else mid if p < last else high


def loop(first, last, body):
    for i in range(first, last):
        body(i)


def halving(rows, cols):
    a = lax.broadcasted_iota(jnp.int32, (rows, cols), 0)
    b = lax.broadcasted_iota(jnp.int32, (rows, cols), 1)
    return flag(a // 2 == b)


def doubling(rows, cols):
    a = lax.broadcasted_iota(jnp.int32, (rows, cols), 0)
    b = lax.broadcasted_iota(jnp.int32, (rows, cols), 1)
    return flag(b // 2 == a)


def dot(a, b):
    b = b.astype(jnp.bfloat16)
    hi = a.astype(jnp.bfloat16)
    a = a - hi.astype(F32)
    mid = a.astype(jnp.bfloat16)
    lo = (a - mid.astype(F32)).astype(jnp.bfloat16)
    one = functools.partial(jnp.dot, preferred_element_type=F32)
    return one(hi, b) + one(mid, b) + one(lo, b)


def turn(tile, by):
    by = by % 128
    return pltpu.roll(tile, by, 1) if by else tile


def x_plane(own, xlo, xhi, p):
    if p < HX:
        return xlo(p)
    return own(p - HX) if p < HX + BX else xhi(p - HX - BX)


def half_tile(src, base, plane):
    at = 4 * (plane % 2)
    return src[base + plane // 2, at : at + 4]


def first_parts(a, own, xlo, xhi, zl, zr, ylo, yhi):
    base = a * 84

    def parts(p):
        g, k = p // 5, p % 5

        def pair(center, left, right):
            lane = lax.broadcasted_iota(jnp.int32, left.shape, 1)
            return center, jnp.where(lane < 64, turn(right, -24 * k), turn(left, 104 - 24 * k))

        whole = lambda y: pair(y[base + p], y[base + 40 + g], y[base + 48 + g])
        half = lambda y: pair(*(half_tile(y, base + 56, m) for m in (p, 40 + g, 48 + g)))
        center = x_plane(lambda i: own[i], lambda i: xlo[a, i], lambda i: xhi[a, i], p)
        middle = pair(center, zl[a, g], zr[a, g])
        return whole(ylo), half(ylo), middle, half(yhi), whole(yhi)

    return parts


def later_parts(own, halo, xlo, xhi, ylo, yhi):
    def parts(p):
        g, k = p // 4, p % 4
        pair = lambda center, side: (center, turn(side, 112 - 32 * k))
        whole = lambda y: pair(y[p], y[40 + g])
        half = lambda y: pair(half_tile(y, 50, p), half_tile(y, 50, 40 + g))
        center = x_plane(lambda i: own[i], lambda i: xlo[i], lambda i: xhi[i], p)
        side = x_plane(
            lambda i: halo[i // 4], lambda i: xlo[12 + i // 4], lambda i: xhi[12 + i // 4], p
        )
        return whole(ylo), half(ylo), pair(center, side), half(yhi), whole(yhi)

    return parts


ROWS = ((0, 8), (8, 12), (12, 44), (44, 48), (48, 56))


def assemble_field(dst, parts):
    gx, gy, gz = places()
    lane = lax.broadcasted_iota(jnp.int32, (1, BZ), 1)
    side = jnp.where(lane < 64, flag(gz < GZ - 1), flag(gz > 0))
    x_low, x_high = flag(gx > 0), flag(gx < GX - 1)
    y_low, y_high = flag(gy > 0), flag(gy < GY - 1)
    for p in range(EX):
        x = x_low if p < HX else None if p < HX + BX else x_high
        for (lo, hi), y, (center, halo) in zip(
            ROWS, (y_low, y_low, None, y_high, y_high), parts(p)
        ):
            scale = x if y is None else y if x is None else x * y
            dst[p, lo:hi, :BZ] = center if scale is None else center * scale
            dst[p, lo:hi, BZ:] = halo * (side if scale is None else side * scale)


def assemble_diagonal(dst, parts):
    for p in range(EX):
        for (lo, hi), (center, halo) in zip(ROWS, parts(p)):
            dst[p, lo:hi, :BZ] = center + 27.0
            dst[p, lo:hi, BZ:] = halo + 27.0


def z_pack_kernel(right_side, diagonal, xlo, xhi, down, up):
    group = lax.broadcasted_iota(jnp.int32, (BY, BZ), 1) // 24
    for a, own in enumerate((right_side, diagonal)):
        for g in range(EX // 5):
            low = high = None
            for k in range(5):
                src = x_plane(
                    lambda i: own[i], lambda i: xlo[a, i], lambda i: xhi[a, i], 5 * g + k
                )
                first, last = turn(src, 24 * k), turn(src, 24 * k - 104)
                low = first if k == 0 else jnp.where(group == k, first, low)
                high = last if k == 0 else jnp.where(group == k, last, high)
            down[a, g] = low
            up[a, g] = high


def y_rows(planes, base, down, up):
    count = len(planes)
    for m, plane in enumerate(planes):
        down[base + m] = plane(4, 12)
        up[base + m] = plane(20, 28)
        at = base + count + m // 2
        row = 4 * (m % 2)
        down[at, row : row + 4] = plane(0, 4)
        up[at, row : row + 4] = plane(28, 32)


def y_pack_kernel(right_side, diagonal, xlo, xhi, zl, zr, down, up):
    def rows(ref, *index):
        return lambda lo, hi: ref[(*index, slice(lo, hi))]

    for a, own in enumerate((right_side, diagonal)):
        planes = [
            x_plane(
                lambda i: rows(own, i), lambda i: rows(xlo, a, i), lambda i: rows(xhi, a, i), p
            )
            for p in range(EX)
        ]
        planes += [rows(zl, a, g) for g in range(8)] + [rows(zr, a, g) for g in range(8)]
        y_rows(planes, 84 * a, down, up)


def y_pack_later_kernel(own, halo, xlo, xhi, down, up):
    def rows(ref, index):
        return lambda lo, hi: ref[index, lo:hi]

    planes = [
        x_plane(lambda i: rows(own, i), lambda i: rows(xlo, i), lambda i: rows(xhi, i), p)
        for p in range(EX)
    ]
    planes += [
        x_plane(
            lambda i: rows(halo, i // 4),
            lambda i: rows(xlo, 12 + i // 4),
            lambda i: rows(xhi, 12 + i // 4),
            4 * g,
        )
        for g in range(10)
    ]
    y_rows(planes, 0, down, up)


def halve(pairs, rows, z_map, dst, scale):
    rows[...] = dot(pairs[...], z_map)
    for p in range(MX):
        at = p * EY
        total = rows[pl.ds(at, MR, stride=2), :] + rows[pl.ds(at + 1, MR, stride=2), :]
        dst[p, :MR] = total * scale
        dst[p, MR:] = jnp.zeros((MY - MR, MZ), F32)


def pre_kernel(first, *refs):
    if first:
        right_side, diagonal, xlo, xhi, zl, zr, ylo, yhi = refs[:8]
        refs = refs[8:]
        assemble_field(refs[7], first_parts(0, right_side, xlo, xhi, zl, zr, ylo, yhi))
    else:
        own, halo, xlo, xhi, ylo, yhi = refs[:6]
        refs = refs[6:]
        assemble_field(refs[7], later_parts(own, halo, xlo, xhi, ylo, yhi))
    d0, d1, zs, rs, z1, left1, packed, field, zfull, pairs, rows, r1, small = refs
    z_map = halving(EZ, MZ)
    if first:
        assemble_diagonal(d0, first_parts(1, diagonal, xlo, xhi, zl, zr, ylo, yhi))
        for i in range(MX):
            pairs[i * EY : (i + 1) * EY, :] = d0[2 * i] + d0[2 * i + 1]
        halve(pairs, rows, z_map, d1, 0.125)
    pairs[0:EY, :] = jnp.zeros((EY, EZ), F32)
    pairs[(MX - 1) * EY :, :] = jnp.zeros((EY, EZ), F32)
    mask = x_masks(plane_mask(0, (EY, EZ), -HY), 0, CA)

    def smooth(p):
        r = field[p]
        box = spread(field[p - 1] + r + field[p + 1])
        z = (CR + CA * d0[p]) * r - mask(p) * box
        zfull[p] = z
        if 10 <= p < 30:
            zs[p - 10] = z[8:48]

    def rest(p):
        z = zfull[p]
        left = field[p] - d0[p] * z + spread(zfull[p - 1] + z + zfull[p + 1])
        if 10 <= p < 30:
            rs[p - 10] = left[8:48]
        return left

    def rest_pair(i):
        pairs[i * EY : (i + 1) * EY, :] = rest(2 * i) + rest(2 * i + 1)

    loop(1, EX - 1, smooth)
    loop(1, MX - 1, rest_pair)
    halve(pairs, rows, z_map, r1, 0.5)
    mask1 = plane_mask(1, (MY, MZ), -HY // 2)
    keep1, mask1 = x_masks(mask1, 1), x_masks(mask1, 1, CA)

    def mask_one(p):
        r1[p] = r1[p] * keep1(p)

    loop(0, MX, mask_one)

    def smooth_one(p):
        r = r1[p]
        box = spread(r1[p - 1] + r + r1[p + 1])
        z1[p] = (CR + CA * d1[p]) * r - mask1(p) * box

    zero = jnp.zeros((MY, MZ), F32)
    for ref in (z1, left1):
        ref[0] = zero
        ref[MX - 1] = zero
    loop(1, MX - 1, smooth_one)

    def rest_one(p):
        z = z1[p]
        left1[p] = r1[p] - d1[p] * z + spread(z1[p - 1] + z + z1[p + 1])

    loop(1, MX - 1, rest_one)

    lane = lax.broadcasted_iota(jnp.int32, (MZ, 128), 0)
    col = lax.broadcasted_iota(jnp.int32, (MZ, 128), 1)

    def pack(src, scale):
        total = jnp.zeros((16, 128), F32)
        for k in range(4):
            s = src[6 + 2 * k, 6:22, :] + src[7 + 2 * k, 6:22, :]
            total = total + dot(s, flag((lane // 2 + 32 * k == col) & (lane < 64)))
        small[...] = total
        return (small[pl.ds(0, 8, stride=2), :] + small[pl.ds(1, 8, stride=2), :]) * scale

    tile = pack(left1, 0.5)
    if first:
        tile = jnp.concatenate([tile, pack(d1, 0.125)], axis=0)
    for i in range(GX * GZ):
        packed[i] = tile


def unpack(dst, row, lo, own, hi):
    group = lax.broadcasted_iota(jnp.int32, (8, 128), 1) // 32
    for part, src in enumerate((lo, own, hi)):
        for bx in range(GX):
            for k in range(4):
                halves = []
                for h in range(2):
                    acc = None
                    for j in range(4):
                        block = src[bx * GZ + 4 * h + j, row : row + 8, :]
                        shift = (32 * (j - k)) % 128
                        if shift:
                            block = pltpu.roll(block, shift, 1)
                        acc = block if acc is None else jnp.where(group == j, block, acc)
                    halves.append(acc)
                dst[1 + 4 * bx + k, 8 * part : 8 * part + 8, :] = jnp.concatenate(halves, axis=1)


def coarse(r2, d2, s0, s1, z2, gy):
    shape = (24, 256)
    row = lax.broadcasted_iota(jnp.int32, shape, 0) + (gy * 8 - 8)
    mask = flag((row >= 0) & (row < 64))
    lane = lax.broadcasted_iota(jnp.int32, shape, 1)

    def box(t):
        t = t + pltpu.roll(t, 1, 0) + pltpu.roll(t, 23, 0)
        return (
            t
            + jnp.where(lane == 0, 0.0, pltpu.roll(t, 1, 1))
            + jnp.where(lane == 255, 0.0, pltpu.roll(t, 255, 1))
        )

    theta, delta = 29.5, 28.5
    sigma = theta / delta
    rho = 1.0 / sigma
    rho1 = 1.0 / (2.0 * sigma - rho)
    rho2 = 1.0 / (2.0 * sigma - rho1)
    zero = jnp.zeros(shape, F32)
    for ref in (r2, s0, s1, z2):
        ref[0] = zero
        ref[17] = zero

    def scale(p):
        r2[p] = r2[p] * mask

    loop(1, 17, scale)

    def one(p):
        r = r2[p]
        step = r * (1.0 / theta)
        remain = mask * (r - d2[p] * step + box(r2[p - 1] + r + r2[p + 1]) * (1.0 / theta))
        s0[p] = remain
        s1[p] = (rho1 * rho) * step + (2.0 * rho1 / delta) * remain

    loop(1, 17, one)

    def two(p):
        step = s1[p]
        remain = mask * (s0[p] - d2[p] * step + box(s1[p - 1] + step + s1[p + 1]))
        last = (rho2 * rho1) * step + (2.0 * rho2 / delta) * remain
        z2[p] = r2[p] * (1.0 / theta) + step + last

    loop(1, 17, two)

    def three(p):
        y = z2[p]
        left = r2[p] - d2[p] * y + box(z2[p - 1] + y + z2[p + 1])
        top = jnp.sum(left, axis=1, keepdims=True)
        low = jnp.sum(d2[p] - 26.0, axis=1, keepdims=True)
        s0[p] = mask * (y + top / low)

    loop(1, 17, three)


def post_kernel(first, *refs):
    if first:
        (lo, own, hi, zs, rs, z1, left1, d0, d1,
         d2, z_core, q_core, q_down, q_up, q_halo,
         r2, s0, s1, z2, wide, rows1, u, rem, zf1, rowsv, v, sv, rem0, zf0) = refs
    else:
        (lo, own, hi, zs, rs, z1, left1, d0, d1, d2,
         z_core, q_core,
         r2, s0, s1, z2, wide, rows1, u, rem, zf1, rowsv, v, sv, rem0, zf0) = refs
    gx, gy, gz = places()
    unpack(r2, 0, lo, own, hi)
    if first:
        unpack(d2, 8, lo, own, hi)
    coarse(r2, d2, s0, s1, z2, gy)

    lane = lax.broadcasted_iota(jnp.int32, (16, 128), 1)
    z = jnp.where(lane < 48, lane, lane - 64) + 32 * gz
    in2 = flag((z >= 0) & (z < 256) & (lane < 64))
    turned = (256 - 32 * gz) % 256
    for i in range(10):
        p = 4 * gx - 3 + i
        plane = pltpu.roll(s0[jnp.clip(p + 1, 0, 17)], turned, 1)[5:21]
        plane = jnp.where(lane < 48, plane[:, :128], turn(plane[:, 128:], 64))
        wide[16 * i : 16 * i + 16, :] = plane * (in2 * flag((p >= 0) & (p < 16)))
    up = dot(wide[...], doubling(128, 128))
    rows1[pl.ds(0, 160, stride=2), :] = up
    rows1[pl.ds(1, 160, stride=2), :] = up
    u[...] = rows1[...].reshape(10, 32, 128)

    mask1 = plane_mask(1, (MY, MZ), -HY // 2)
    keep1, mask1 = x_masks(mask1, 1), x_masks(mask1, 1, CA)

    def remain_one(p):
        c = u[p // 2]
        total = u[(p - 1) // 2] + c + u[(p + 1) // 2]
        rem[p] = keep1(p) * (left1[p] - d1[p] * c + spread(total))

    loop(3, 17, remain_one)

    def final_one(p):
        r = rem[p]
        box = spread(rem[p - 1] + r + rem[p + 1])
        f = z1[p] + u[p // 2] + ((CR + CA * d1[p]) * r - mask1(p) * box)
        zf1[(p - 4) * 20 : (p - 3) * 20, :] = f[4:24]

    loop(4, 16, final_one)

    rowsv[pl.ds(0, 240, stride=2), :] = zf1[...]
    rowsv[pl.ds(1, 240, stride=2), :] = zf1[...]
    v[...] = dot(rowsv[...], doubling(128, 256)).reshape(12, PY, EZ)
    for i in range(12):
        sv[i] = spread(v[i])

    mask0 = plane_mask(0, (PY, EZ), -4)
    keep0, mask0 = x_masks(mask0, 0), x_masks(mask0, 0, CA)

    def remain(i):
        p = i + 10
        at = p // 2 - 4
        other = (p - 1) // 2 - 4 if p % 2 == 0 else (p + 1) // 2 - 4
        rem0[i] = keep0(p) * (rs[i] - d0[p, 8:48, :] * v[at] + (2.0 * sv[at] + sv[other]))

    loop(0, 20, remain)

    def final(i):
        p = i + 10
        r = rem0[i]
        box = spread(rem0[i - 1] + r + rem0[i + 1])
        zf0[i] = zs[i] + v[p // 2 - 4] + ((CR + CA * d0[p, 8:48, :]) * r - mask0(p) * box)

    loop(1, 19, final)

    group = lax.broadcasted_iota(jnp.int32, (BY, BZ), 1) // 32

    def apply(i):
        c = zf0[i + 2]
        q = d0[i + HX, 8:48, :] * c - spread(zf0[i + 1] + c + zf0[i + 3])
        q_own = q[4:36, :BZ]
        z_core[i] = c[4:36, :BZ]
        q_core[i] = q_own
        if first:
            if i < 12:
                q_down[i] = q_own
            if i >= 4:
                q_up[i - 4] = q_own
            g, k = i // 4, i % 4
            halo = turn(q[4:36, BZ:], 32 * k - 112)
            if k:
                halo = jnp.where(group == k, halo, q_halo[g])
            q_halo[g] = halo
            if k == 3 and g < 3:
                q_down[12 + g] = halo
            if k == 3 and g > 0:
                q_up[11 + g] = halo

    loop(0, BX, apply)


def dots_kernel(r, z, q, p, w, dots):
    acc = [None] * 9
    for i in range(BX):
        ri, zi, qi, pi, wi = r[i], z[i], q[i], p[i], w[i]
        r1, z1, w1 = ri - qi, zi - pi, qi - wi
        terms = (
            ri * zi, zi * qi, r1 * z1, r1 * pi + qi * z1, qi * pi,
            z1 * w1, z1 * wi + pi * w1, pi * wi, z1 * qi,
        )
        for k, term in enumerate(terms):
            acc[k] = term if i == 0 else acc[k] + term
    lane = lax.broadcasted_iota(jnp.int32, (1, 128), 1)
    row = jnp.zeros((1, 128), F32)
    for k, part in enumerate(acc):
        total = jnp.sum(jnp.sum(part, axis=0, keepdims=True), axis=1, keepdims=True)
        row = jnp.where(lane == k, total, row)
    dots[...] = jnp.broadcast_to(row[None], (GY * GZ, 1, 128))


def end_kernel(r, z, q, p, w, m0, m1, m2, m3, solution_field, residual):
    last = jnp.sum(m0[...] + m1[...] + m2[...] + m3[...], axis=0)
    lane = lax.broadcasted_iota(jnp.int32, (1, 128), 1)
    at = lambda i: jnp.sum(jnp.where(lane == i, last, 0.0), axis=1, keepdims=True)
    rz, curve = at(0), at(1)
    alpha = rz / curve
    t = alpha - 1.0
    rz2 = at(2) - t * at(3) + t * t * at(4)
    zw = at(5) - t * at(6) + t * t * at(7)
    zq = at(8) - t * at(4)
    beta = rz2 / rz
    alpha2 = rz2 / (zw + 2.0 * beta * zq + beta * beta * curve)

    def body(i):
        zi, qi = z[i], q[i]
        solution_field[i] = alpha * zi + alpha2 * ((zi - alpha * p[i]) + beta * zi)
        residual[i] = (r[i] - alpha * qi) - alpha2 * ((qi - alpha * w[i]) + beta * qi)

    loop(0, BX, body)


def shape(*dims):
    return jax.ShapeDtypeStruct(dims, F32)


def call(kernel, outs, scratch, *args):
    whole = pl.BlockSpec(memory_space=pltpu.VMEM)
    return pl.pallas_call(
        kernel,
        out_shape=outs,
        in_specs=[whole] * len(args),
        out_specs=jax.tree.map(lambda _: whole, outs),
        scratch_shapes=[pltpu.VMEM(s, F32) for s in scratch],
        compiler_params=pltpu.CompilerParams(vmem_limit_bytes=24 * 1024 * 1024),
    )(*args)


def shift(value, axis, count, by):
    return lax.ppermute(value, axis, [(i, (i + by) % count) for i in range(count)])


def spread_coarse(packed):
    own = lax.all_to_all(packed, ("gx", "gz"), 0, 0)
    return shift(own, "gy", GY, 1), own, shift(own, "gy", GY, -1)


def pre_call(first, *args):
    kept = (shape(20, PY, EZ), shape(20, PY, EZ), shape(MX, MY, MZ), shape(MX, MY, MZ),
            shape(GX * GZ, 16 if first else 8, 128))
    scratch = [(EX, EY, EZ), (EX, EY, EZ), (MX * EY, EZ), (MX * EY, MZ), (MX, MY, MZ), (16, 128)]
    kernel = functools.partial(pre_kernel, first)
    if first:
        kept = (shape(EX, EY, EZ), shape(MX, MY, MZ)) + kept
    return call(kernel, kept, scratch, *args)


def post_call(parts, kept, d0, d1, d2=None):
    first = d2 is None
    scratch = [(18, 24, 256)] * 4 + [
        (160, 128), (320, 128), (10, 32, 128), (MX, MY, MZ), (240, 128),
        (480, 128), (12, PY, EZ), (12, PY, EZ), (20, PY, EZ), (20, PY, EZ),
    ]
    core = shape(BX, BY, BZ)
    kernel = functools.partial(post_kernel, first)
    if first:
        slab = shape(15, BY, BZ)
        outs = (shape(18, 24, 256), core, core, slab, slab, shape(4, BY, BZ))
        return call(kernel, outs, scratch, *parts, *kept, d0, d1)
    return call(kernel, (core, core), scratch, *parts, *kept, d0, d1, d2)


def first_exchange(right_side, diagonal):
    def slab(lo, hi):
        return jnp.stack([right_side[lo:hi], diagonal[lo:hi]])

    xlo = shift(slab(BX - HX, BX), "gx", GX, 1)
    xhi = shift(slab(0, HX), "gx", GX, -1)
    edge = shape(2, EX // 5, BY, BZ)
    down, up = call(z_pack_kernel, (edge, edge), [], right_side, diagonal, xlo, xhi)
    zl = shift(up, "gz", GZ, 1)
    zr = shift(down, "gz", GZ, -1)
    edge = shape(168, 8, BZ)
    pieces = (right_side, diagonal, xlo, xhi, zl, zr)
    down, up = call(y_pack_kernel, (edge, edge), [], *pieces)
    return *pieces, shift(up, "gy", GY, 1), shift(down, "gy", GY, -1)


def later_exchange(q, q_down, q_up, q_halo):
    xlo = shift(q_up, "gx", GX, 1)
    xhi = shift(q_down, "gx", GX, -1)
    edge = shape(75, 8, BZ)
    down, up = call(y_pack_later_kernel, (edge, edge), [], q, q_halo, xlo, xhi)
    return q, q_halo, xlo, xhi, shift(up, "gy", GY, 1), shift(down, "gy", GY, -1)


def local(right_side, diagonal):
    d0, d1, *kept = pre_call(True, *first_exchange(right_side, diagonal))
    d2, z, q, *edges = post_call(spread_coarse(kept[-1]), kept[:-1], d0, d1)
    kept = pre_call(False, *later_exchange(q, *edges), d0, d1)
    p, w = post_call(spread_coarse(kept[-1]), kept[:-1], d0, d1, d2=d2)
    fields = (right_side, z, q, p, w)
    more = call(dots_kernel, shape(GY * GZ, 1, 128), [], *fields)
    more = lax.all_to_all(more, ("gy", "gz"), 0, 0)
    others = [shift(more, "gx", GX, i) for i in (1, 2, 3)]
    core = shape(BX, BY, BZ)
    return call(end_kernel, (core, core), [], *fields, more, *others)


def solution(mesh):
    return jax.shard_map(
        local, mesh=mesh, in_specs=(SPEC, SPEC), out_specs=(SPEC, SPEC), check_vma=False
    )
```

```python
import functools

import jax
import jax.numpy as jnp
from jax import lax
from jax.experimental import pallas as pl
from jax.experimental.pallas import tpu as pltpu
from jax.sharding import PartitionSpec as P

GX, GY, GZ = 4, 8, 8
BX, BY, BZ = 16, 32, 128
HX, HY = 12, 12
EX, EY, EZ = BX + 2 * HX, BY + 2 * HY, 2 * BZ
MX, MR, MY, MZ = EX // 2, EY // 2, 32, BZ
PY = BY + 8
F32 = jnp.float32
SPEC = P("gx", "gy", "gz")


def cheb_two(lower, upper=58.0):
    theta, delta = (upper + lower) / 2.0, (upper - lower) / 2.0
    sigma = theta / delta
    rho = 1.0 / sigma
    after = 1.0 / (2.0 * sigma - rho)
    return (1.0 + after * rho) / theta + 2.0 * after / delta, -2.0 * after / (delta * theta)


CR, CA = cheb_two(7.0)


def spread(t):
    t = t + pltpu.roll(t, 1, 0) + pltpu.roll(t, t.shape[0] - 1, 0)
    return t + pltpu.roll(t, 1, 1) + pltpu.roll(t, t.shape[1] - 1, 1)


def flag(condition):
    return jnp.where(condition, 1.0, 0.0).astype(F32)


def places():
    return lax.axis_index("gx"), lax.axis_index("gy"), lax.axis_index("gz")


def plane_mask(level, shape, row):
    _, gy, gz = places()
    size = 1 << level
    y = lax.broadcasted_iota(jnp.int32, shape, 0) + (gy * (BY // size) + row)
    lane = lax.broadcasted_iota(jnp.int32, shape, 1)
    z = jnp.where(lane < 3 * shape[1] // 4, lane, lane - shape[1]) + gz * (BZ // size)
    return flag((y >= 0) & (y < GY * BY // size) & (z >= 0) & (z < GZ * BZ // size))


def x_masks(mask, level, scale=1.0):
    gx = places()[0]
    first, last = HX >> level, (HX + BX) >> level
    low, high = flag(gx > 0) * scale, flag(gx < GX - 1) * scale
    low, mid, high = mask * low, mask * scale, mask * high
    return lambda p: low if p < first else mid if p < last else high


def loop(first, last, body):
    for i in range(first, last):
        body(i)


def halving(rows, cols):
    a = lax.broadcasted_iota(jnp.int32, (rows, cols), 0)
    b = lax.broadcasted_iota(jnp.int32, (rows, cols), 1)
    return flag(a // 2 == b)


def doubling(rows, cols):
    a = lax.broadcasted_iota(jnp.int32, (rows, cols), 0)
    b = lax.broadcasted_iota(jnp.int32, (rows, cols), 1)
    return flag(b // 2 == a)


def dot(a, b):
    b = b.astype(jnp.bfloat16)
    hi = a.astype(jnp.bfloat16)
    a = a - hi.astype(F32)
    mid = a.astype(jnp.bfloat16)
    lo = (a - mid.astype(F32)).astype(jnp.bfloat16)
    one = functools.partial(jnp.dot, preferred_element_type=F32)
    return one(hi, b) + one(mid, b) + one(lo, b)


def turn(tile, by):
    by = by % 128
    return pltpu.roll(tile, by, 1) if by else tile


def x_plane(own, xlo, xhi, p):
    if p < HX:
        return xlo(p)
    return own(p - HX) if p < HX + BX else xhi(p - HX - BX)


def half_tile(src, base, plane):
    at = 4 * (plane % 2)
    return src[base + plane // 2, at : at + 4]


def first_parts(a, own, xlo, xhi, zl, zr, ylo, yhi):
    base = a * 84

    def parts(p):
        g, k = p // 5, p % 5

        def pair(center, left, right):
            lane = lax.broadcasted_iota(jnp.int32, left.shape, 1)
            return center, jnp.where(lane < 64, turn(right, -24 * k), turn(left, 104 - 24 * k))

        whole = lambda y: pair(y[base + p], y[base + 40 + g], y[base + 48 + g])
        half = lambda y: pair(*(half_tile(y, base + 56, m) for m in (p, 40 + g, 48 + g)))
        center = x_plane(lambda i: own[i], lambda i: xlo[a, i], lambda i: xhi[a, i], p)
        middle = pair(center, zl[a, g], zr[a, g])
        return whole(ylo), half(ylo), middle, half(yhi), whole(yhi)

    return parts


def later_parts(own, halo, xlo, xhi, ylo, yhi):
    def parts(p):
        g, k = p // 4, p % 4
        pair = lambda center, side: (center, turn(side, 112 - 32 * k))
        whole = lambda y: pair(y[p], y[40 + g])
        half = lambda y: pair(half_tile(y, 50, p), half_tile(y, 50, 40 + g))
        center = x_plane(lambda i: own[i], lambda i: xlo[i], lambda i: xhi[i], p)
        side = x_plane(
            lambda i: halo[i // 4], lambda i: xlo[12 + i // 4], lambda i: xhi[12 + i // 4], p
        )
        return whole(ylo), half(ylo), pair(center, side), half(yhi), whole(yhi)

    return parts


ROWS = ((0, 8), (8, 12), (12, 44), (44, 48), (48, 56))


def assemble_field(dst, parts):
    gx, gy, gz = places()
    lane = lax.broadcasted_iota(jnp.int32, (1, BZ), 1)
    side = jnp.where(lane < 64, flag(gz < GZ - 1), flag(gz > 0))
    x_low, x_high = flag(gx > 0), flag(gx < GX - 1)
    y_low, y_high = flag(gy > 0), flag(gy < GY - 1)
    for p in range(EX):
        x = x_low if p < HX else None if p < HX + BX else x_high
        for (lo, hi), y, (center, halo) in zip(
            ROWS, (y_low, y_low, None, y_high, y_high), parts(p)
        ):
            scale = x if y is None else y if x is None else x * y
            dst[p, lo:hi, :BZ] = center if scale is None else center * scale
            dst[p, lo:hi, BZ:] = halo * (side if scale is None else side * scale)


def assemble_diagonal(dst, parts):
    for p in range(EX):
        for (lo, hi), (center, halo) in zip(ROWS, parts(p)):
            dst[p, lo:hi, :BZ] = center + 27.0
            dst[p, lo:hi, BZ:] = halo + 27.0


def z_pack_kernel(right_side, diagonal, xlo, xhi, down, up):
    group = lax.broadcasted_iota(jnp.int32, (BY, BZ), 1) // 24
    for a, own in enumerate((right_side, diagonal)):
        for g in range(EX // 5):
            low = high = None
            for k in range(5):
                src = x_plane(
                    lambda i: own[i], lambda i: xlo[a, i], lambda i: xhi[a, i], 5 * g + k
                )
                first, last = turn(src, 24 * k), turn(src, 24 * k - 104)
                low = first if k == 0 else jnp.where(group == k, first, low)
                high = last if k == 0 else jnp.where(group == k, last, high)
            down[a, g] = low
            up[a, g] = high


def y_rows(planes, base, down, up):
    count = len(planes)
    for m, plane in enumerate(planes):
        down[base + m] = plane(4, 12)
        up[base + m] = plane(20, 28)
        at = base + count + m // 2
        row = 4 * (m % 2)
        down[at, row : row + 4] = plane(0, 4)
        up[at, row : row + 4] = plane(28, 32)


def y_pack_kernel(right_side, diagonal, xlo, xhi, zl, zr, down, up):
    def rows(ref, *index):
        return lambda lo, hi: ref[(*index, slice(lo, hi))]

    for a, own in enumerate((right_side, diagonal)):
        planes = [
            x_plane(
                lambda i: rows(own, i), lambda i: rows(xlo, a, i), lambda i: rows(xhi, a, i), p
            )
            for p in range(EX)
        ]
        planes += [rows(zl, a, g) for g in range(8)] + [rows(zr, a, g) for g in range(8)]
        y_rows(planes, 84 * a, down, up)


def y_pack_later_kernel(own, halo, xlo, xhi, down, up):
    def rows(ref, index):
        return lambda lo, hi: ref[index, lo:hi]

    planes = [
        x_plane(lambda i: rows(own, i), lambda i: rows(xlo, i), lambda i: rows(xhi, i), p)
        for p in range(EX)
    ]
    planes += [
        x_plane(
            lambda i: rows(halo, i // 4),
            lambda i: rows(xlo, 12 + i // 4),
            lambda i: rows(xhi, 12 + i // 4),
            4 * g,
        )
        for g in range(10)
    ]
    y_rows(planes, 0, down, up)


def halve(pairs, rows, z_map, dst, scale):
    rows[...] = dot(pairs[...], z_map)
    for p in range(MX):
        at = p * EY
        total = rows[pl.ds(at, MR, stride=2), :] + rows[pl.ds(at + 1, MR, stride=2), :]
        dst[p, :MR] = total * scale
        dst[p, MR:] = jnp.zeros((MY - MR, MZ), F32)


def pre_kernel(first, *refs):
    if first:
        right_side, diagonal, xlo, xhi, zl, zr, ylo, yhi = refs[:8]
        refs = refs[8:]
        assemble_field(refs[7], first_parts(0, right_side, xlo, xhi, zl, zr, ylo, yhi))
    else:
        own, halo, xlo, xhi, ylo, yhi = refs[:6]
        refs = refs[6:]
        assemble_field(refs[7], later_parts(own, halo, xlo, xhi, ylo, yhi))
    d0, d1, zs, rs, z1, left1, packed, field, zfull, pairs, rows, r1, small = refs
    z_map = halving(EZ, MZ)
    if first:
        assemble_diagonal(d0, first_parts(1, diagonal, xlo, xhi, zl, zr, ylo, yhi))
        for i in range(MX):
            pairs[i * EY : (i + 1) * EY, :] = d0[2 * i] + d0[2 * i + 1]
        halve(pairs, rows, z_map, d1, 0.125)
    pairs[0:EY, :] = jnp.zeros((EY, EZ), F32)
    pairs[(MX - 1) * EY :, :] = jnp.zeros((EY, EZ), F32)
    mask = x_masks(plane_mask(0, (EY, EZ), -HY), 0, CA)

    def smooth(p):
        r = field[p]
        box = spread(field[p - 1] + r + field[p + 1])
        z = (CR + CA * d0[p]) * r - mask(p) * box
        zfull[p] = z
        if 10 <= p < 30:
            zs[p - 10] = z[8:48]

    def rest(p):
        z = zfull[p]
        left = field[p] - d0[p] * z + spread(zfull[p - 1] + z + zfull[p + 1])
        if 10 <= p < 30:
            rs[p - 10] = left[8:48]
        return left

    def rest_pair(i):
        pairs[i * EY : (i + 1) * EY, :] = rest(2 * i) + rest(2 * i + 1)

    loop(1, EX - 1, smooth)
    loop(1, MX - 1, rest_pair)
    halve(pairs, rows, z_map, r1, 0.5)
    mask1 = plane_mask(1, (MY, MZ), -HY // 2)
    keep1, mask1 = x_masks(mask1, 1), x_masks(mask1, 1, CA)

    def mask_one(p):
        r1[p] = r1[p] * keep1(p)

    loop(0, MX, mask_one)

    def smooth_one(p):
        r = r1[p]
        box = spread(r1[p - 1] + r + r1[p + 1])
        z1[p] = (CR + CA * d1[p]) * r - mask1(p) * box

    zero = jnp.zeros((MY, MZ), F32)
    for ref in (z1, left1):
        ref[0] = zero
        ref[MX - 1] = zero
    loop(1, MX - 1, smooth_one)

    def rest_one(p):
        z = z1[p]
        left1[p] = r1[p] - d1[p] * z + spread(z1[p - 1] + z + z1[p + 1])

    loop(1, MX - 1, rest_one)

    lane = lax.broadcasted_iota(jnp.int32, (MZ, 128), 0)
    col = lax.broadcasted_iota(jnp.int32, (MZ, 128), 1)

    def pack(src, scale):
        total = jnp.zeros((16, 128), F32)
        for k in range(4):
            s = src[6 + 2 * k, 6:22, :] + src[7 + 2 * k, 6:22, :]
            total = total + dot(s, flag((lane // 2 + 32 * k == col) & (lane < 64)))
        small[...] = total
        return (small[pl.ds(0, 8, stride=2), :] + small[pl.ds(1, 8, stride=2), :]) * scale

    tile = pack(left1, 0.5)
    if first:
        tile = jnp.concatenate([tile, pack(d1, 0.125)], axis=0)
    for i in range(GX * GZ):
        packed[i] = tile


def unpack(dst, row, lo, own, hi, scales):
    group = lax.broadcasted_iota(jnp.int32, (8, 128), 1) // 32
    for part, (src, scale) in enumerate(zip((lo, own, hi), scales)):
        for bx in range(GX):
            for k in range(4):
                for h in range(2):
                    acc = None
                    for j in range(4):
                        block = turn(src[bx * GZ + 4 * h + j, row : row + 8, :], 32 * (j - k))
                        acc = block if acc is None else jnp.where(group == j, block, acc)
                    rows = slice(8 * part, 8 * part + 8)
                    lanes = slice(128 * h, 128 * h + 128)
                    dst[6 + 4 * bx + k, rows, lanes] = acc if scale is None else acc * scale
    for p in (*range(6), *range(22, 28)):
        dst[p] = jnp.zeros((24, 256), F32)


def coarse(r2, d2, s0, s1, z2):
    gx, gy, _ = places()
    shape = (24, 256)
    row = lax.broadcasted_iota(jnp.int32, shape, 0) + (gy * 8 - 8)
    mask = flag((row >= 0) & (row < 64))
    low, high = mask * flag(gx > 0), mask * flag(gx < GX - 1)
    inside = lambda i: low if i < 6 else mask if i < 10 else high
    lane = lax.broadcasted_iota(jnp.int32, shape, 1)
    at = lambda ref, i: ref[4 * gx + i]

    def box(t):
        t = t + pltpu.roll(t, 1, 0) + pltpu.roll(t, 23, 0)
        return (
            t
            + jnp.where(lane == 0, 0.0, pltpu.roll(t, 1, 1))
            + jnp.where(lane == 255, 0.0, pltpu.roll(t, 255, 1))
        )

    theta, delta = 29.5, 28.5
    sigma = theta / delta
    rho = 1.0 / sigma
    rho1 = 1.0 / (2.0 * sigma - rho)
    rho2 = 1.0 / (2.0 * sigma - rho1)

    for i in range(2, 14):
        r = at(r2, i)
        step = r * (1.0 / theta)
        total = box(at(r2, i - 1) + r + at(r2, i + 1)) * (1.0 / theta)
        remain = inside(i) * (r - at(d2, i) * step + total)
        s0[i] = remain
        s1[i] = (rho1 * rho) * step + (2.0 * rho1 / delta) * remain
    for i in range(3, 13):
        step = s1[i]
        remain = inside(i) * (s0[i] - at(d2, i) * step + box(s1[i - 1] + step + s1[i + 1]))
        last = (rho2 * rho1) * step + (2.0 * rho2 / delta) * remain
        z2[i] = at(r2, i) * (1.0 / theta) + step + last
    for i in range(4, 12):
        y, d = z2[i], at(d2, i)
        left = at(r2, i) - d * y + box(z2[i - 1] + y + z2[i + 1])
        top = jnp.sum(left, axis=1, keepdims=True)
        bottom = jnp.sum(d - 26.0, axis=1, keepdims=True)
        s0[i] = inside(i) * (y + top / bottom)


def post_kernel(first, *refs):
    lo, own, hi, zs, rs, z1, left1, d0, d1 = refs[:9]
    if first:
        d2, z_core, q_core, q_down, q_up, q_halo = refs[9:15]
    else:
        d2, r_old, z_old, q_old, z_core, q_core, dots = refs[9:16]
    r2, s0, s1, z2, wide, rows1, u, rem, zf1, rowsv, v, sv, rem0, zf0 = refs[-14:]
    gx, gy, gz = places()
    scales = (flag(gy > 0), None, flag(gy < GY - 1))
    unpack(r2, 0, lo, own, hi, scales)
    if first:
        unpack(d2, 8, lo, own, hi, (None, None, None))
    coarse(r2, d2, s0, s1, z2)

    lane = lax.broadcasted_iota(jnp.int32, (16, 128), 1)
    z = jnp.where(lane < 48, lane, lane - 64) + 32 * gz
    in2 = flag((z >= 0) & (z < 256) & (lane < 64))
    turned = (256 - 32 * gz) % 256
    for i in range(8):
        plane = pltpu.roll(s0[i + 4], turned, 1)[5:21]
        plane = jnp.where(lane < 48, plane[:, :128], turn(plane[:, 128:], 64))
        wide[16 * i : 16 * i + 16, :] = plane * in2
    up = dot(wide[...], doubling(128, 128))
    rows1[pl.ds(0, 128, stride=2), :] = up
    rows1[pl.ds(1, 128, stride=2), :] = up
    u[1:9] = rows1[...].reshape(8, 32, 128)

    mask1 = plane_mask(1, (MY, MZ), -HY // 2)
    keep1, mask1 = x_masks(mask1, 1), x_masks(mask1, 1, CA)

    def remain_one(p):
        c = u[p // 2]
        total = u[(p - 1) // 2] + c + u[(p + 1) // 2]
        rem[p] = keep1(p) * (left1[p] - d1[p] * c + spread(total))

    loop(3, 17, remain_one)

    def final_one(p):
        r = rem[p]
        box = spread(rem[p - 1] + r + rem[p + 1])
        f = z1[p] + u[p // 2] + ((CR + CA * d1[p]) * r - mask1(p) * box)
        zf1[(p - 4) * 20 : (p - 3) * 20, :] = f[4:24]

    loop(4, 16, final_one)

    rowsv[pl.ds(0, 240, stride=2), :] = zf1[...]
    rowsv[pl.ds(1, 240, stride=2), :] = zf1[...]
    v[...] = dot(rowsv[...], doubling(128, 256)).reshape(12, PY, EZ)
    for i in range(12):
        sv[i] = spread(v[i])

    mask0 = plane_mask(0, (PY, EZ), -4)
    keep0, mask0 = x_masks(mask0, 0), x_masks(mask0, 0, CA)

    def remain(i):
        p = i + 10
        at = p // 2 - 4
        other = (p - 1) // 2 - 4 if p % 2 == 0 else (p + 1) // 2 - 4
        rem0[i] = keep0(p) * (rs[i] - d0[p, 8:48, :] * v[at] + (2.0 * sv[at] + sv[other]))

    loop(0, 20, remain)

    def final(i):
        p = i + 10
        r = rem0[i]
        box = spread(rem0[i - 1] + r + rem0[i + 1])
        zf0[i] = zs[i] + v[p // 2 - 4] + ((CR + CA * d0[p, 8:48, :]) * r - mask0(p) * box)

    loop(1, 19, final)

    group = lax.broadcasted_iota(jnp.int32, (BY, BZ), 1) // 32
    acc = [None] * 9

    def apply(i):
        c = zf0[i + 2]
        q = d0[i + HX, 8:48, :] * c - spread(zf0[i + 1] + c + zf0[i + 3])
        q_own, z_own = q[4:36, :BZ], c[4:36, :BZ]
        z_core[i] = z_own
        q_core[i] = q_own
        if not first:
            for k, term in enumerate(products(r_old[i], z_old[i], q_old[i], z_own, q_own)):
                term = term[:8] + term[8:16] + (term[16:24] + term[24:])
                acc[k] = term if i == 0 else acc[k] + term
        if first:
            if i < 12:
                q_down[i] = q_own
            if i >= 4:
                q_up[i - 4] = q_own
            g, k = i // 4, i % 4
            halo = turn(q[4:36, BZ:], 32 * k - 112)
            if k:
                halo = jnp.where(group == k, halo, q_halo[g])
            q_halo[g] = halo
            if k == 3 and g < 3:
                q_down[12 + g] = halo
            if k == 3 and g > 0:
                q_up[11 + g] = halo

    loop(0, BX, apply)
    if not first:
        lane = lax.broadcasted_iota(jnp.int32, (1, 128), 1)
        row = jnp.zeros((1, 128), F32)
        for k, part in enumerate(acc):
            total = jnp.sum(jnp.sum(part, axis=0, keepdims=True), axis=1, keepdims=True)
            row = jnp.where(lane == k, total, row)
        dots[...] = jnp.broadcast_to(row[None], dots.shape)


def products(r, z, q, p, w):
    r1, z1, w1 = r - q, z - p, q - w
    return (
        r * z, z * q, r1 * z1, r1 * p + q * z1, q * p, z1 * w1, z1 * w + p * w1, p * w, z1 * q,
    )


def end_kernel(r, z, q, p, w, sums, solution_field, residual):
    last = jnp.sum(sums[...], axis=0)
    lane = lax.broadcasted_iota(jnp.int32, (1, 128), 1)
    at = lambda i: jnp.sum(jnp.where(lane == i, last, 0.0), axis=1, keepdims=True)
    rz, curve = at(0), at(1)
    alpha = rz / curve
    t = alpha - 1.0
    rz2 = at(2) - t * at(3) + t * t * at(4)
    zw = at(5) - t * at(6) + t * t * at(7)
    zq = at(8) - t * at(4)
    beta = rz2 / rz
    alpha2 = rz2 / (zw + 2.0 * beta * zq + beta * beta * curve)

    def body(i):
        zi, qi = z[i], q[i]
        solution_field[i] = alpha * zi + alpha2 * ((zi - alpha * p[i]) + beta * zi)
        residual[i] = (r[i] - alpha * qi) - alpha2 * ((qi - alpha * w[i]) + beta * qi)

    loop(0, BX, body)


def shape(*dims):
    return jax.ShapeDtypeStruct(dims, F32)


def call(kernel, outs, scratch, *args):
    whole = pl.BlockSpec(memory_space=pltpu.VMEM)
    return pl.pallas_call(
        kernel,
        out_shape=outs,
        in_specs=[whole] * len(args),
        out_specs=jax.tree.map(lambda _: whole, outs),
        scratch_shapes=[pltpu.VMEM(s, F32) for s in scratch],
        compiler_params=pltpu.CompilerParams(vmem_limit_bytes=24 * 1024 * 1024),
    )(*args)


def shift(value, axis, count, by):
    return lax.ppermute(value, axis, [(i, (i + by) % count) for i in range(count)])


def spread_coarse(packed):
    own = lax.all_to_all(packed, ("gx", "gz"), 0, 0)
    return shift(own, "gy", GY, 1), own, shift(own, "gy", GY, -1)


def pre_call(first, *args):
    kept = (shape(20, PY, EZ), shape(20, PY, EZ), shape(MX, MY, MZ), shape(MX, MY, MZ),
            shape(GX * GZ, 16 if first else 8, 128))
    scratch = [(EX, EY, EZ), (EX, EY, EZ), (MX * EY, EZ), (MX * EY, MZ), (MX, MY, MZ), (16, 128)]
    kernel = functools.partial(pre_kernel, first)
    if first:
        kept = (shape(EX, EY, EZ), shape(MX, MY, MZ)) + kept
    return call(kernel, kept, scratch, *args)


def post_call(parts, kept, d0, d1, *old):
    first = not old
    scratch = [(28, 24, 256)] + [(16, 24, 256)] * 3 + [
        (128, 128), (256, 128), (10, 32, 128), (MX, MY, MZ), (240, 128),
        (480, 128), (12, PY, EZ), (12, PY, EZ), (20, PY, EZ), (20, PY, EZ),
    ]
    core = shape(BX, BY, BZ)
    kernel = functools.partial(post_kernel, first)
    if first:
        slab = shape(15, BY, BZ)
        outs = (shape(28, 24, 256), core, core, slab, slab, shape(4, BY, BZ))
        return call(kernel, outs, scratch, *parts, *kept, d0, d1)
    outs = (core, core, shape(GX * GY * GZ, 1, 128))
    return call(kernel, outs, scratch, *parts, *kept, d0, d1, *old)


def first_exchange(right_side, diagonal):
    def slab(lo, hi):
        return jnp.stack([right_side[lo:hi], diagonal[lo:hi]])

    xlo = shift(slab(BX - HX, BX), "gx", GX, 1)
    xhi = shift(slab(0, HX), "gx", GX, -1)
    edge = shape(2, EX // 5, BY, BZ)
    down, up = call(z_pack_kernel, (edge, edge), [], right_side, diagonal, xlo, xhi)
    zl = shift(up, "gz", GZ, 1)
    zr = shift(down, "gz", GZ, -1)
    edge = shape(168, 8, BZ)
    pieces = (right_side, diagonal, xlo, xhi, zl, zr)
    down, up = call(y_pack_kernel, (edge, edge), [], *pieces)
    return *pieces, shift(up, "gy", GY, 1), shift(down, "gy", GY, -1)


def later_exchange(q, q_down, q_up, q_halo):
    xlo = shift(q_up, "gx", GX, 1)
    xhi = shift(q_down, "gx", GX, -1)
    edge = shape(75, 8, BZ)
    down, up = call(y_pack_later_kernel, (edge, edge), [], q, q_halo, xlo, xhi)
    return q, q_halo, xlo, xhi, shift(up, "gy", GY, 1), shift(down, "gy", GY, -1)


def local(right_side, diagonal):
    d0, d1, *kept = pre_call(True, *first_exchange(right_side, diagonal))
    d2, z, q, *edges = post_call(spread_coarse(kept[-1]), kept[:-1], d0, d1)
    kept = pre_call(False, *later_exchange(q, *edges), d0, d1)
    p, w, dots = post_call(
        spread_coarse(kept[-1]), kept[:-1], d0, d1, d2, right_side, z, q
    )
    sums = lax.all_to_all(dots, ("gx", "gy", "gz"), 0, 0)
    core = shape(BX, BY, BZ)
    return call(end_kernel, (core, core), [], right_side, z, q, p, w, sums)


def solution(mesh):
    return jax.shard_map(
        local, mesh=mesh, in_specs=(SPEC, SPEC), out_specs=(SPEC, SPEC), check_vma=False
    )
```

```python
import functools

import jax
import jax.numpy as jnp
from jax import lax
from jax.experimental import pallas as pl
from jax.experimental.pallas import tpu as pltpu
from jax.sharding import PartitionSpec as P

GX, GY, GZ = 4, 8, 8
BX, BY, BZ = 16, 32, 128
HX, HY = 12, 12
EX, EY, EZ = BX + 2 * HX, BY + 2 * HY, 2 * BZ
MX, MR, MY, MZ = EX // 2, EY // 2, 32, BZ
PY = BY + 8
F32 = jnp.float32
SPEC = P("gx", "gy", "gz")


def cheb_two(lower, upper=58.0):
    theta, delta = (upper + lower) / 2.0, (upper - lower) / 2.0
    sigma = theta / delta
    rho = 1.0 / sigma
    after = 1.0 / (2.0 * sigma - rho)
    return (1.0 + after * rho) / theta + 2.0 * after / delta, -2.0 * after / (delta * theta)


CR, CA = cheb_two(7.0)


def spread_y(t):
    return t + pltpu.roll(t, 1, 0) + pltpu.roll(t, t.shape[0] - 1, 0)


def spread_z(t):
    return t + pltpu.roll(t, 1, 1) + pltpu.roll(t, t.shape[1] - 1, 1)


def spread(t):
    return spread_z(spread_y(t))


def flag(condition):
    return jnp.where(condition, 1.0, 0.0).astype(F32)


def places():
    return lax.axis_index("gx"), lax.axis_index("gy"), lax.axis_index("gz")


def plane_mask(level, shape, row):
    _, gy, gz = places()
    size = 1 << level
    y = lax.broadcasted_iota(jnp.int32, shape, 0) + (gy * (BY // size) + row)
    lane = lax.broadcasted_iota(jnp.int32, shape, 1)
    z = jnp.where(lane < 3 * shape[1] // 4, lane, lane - shape[1]) + gz * (BZ // size)
    return flag((y >= 0) & (y < GY * BY // size) & (z >= 0) & (z < GZ * BZ // size))


def x_masks(mask, level, scale=1.0):
    gx = places()[0]
    first, last = HX >> level, (HX + BX) >> level
    low, high = flag(gx > 0) * scale, flag(gx < GX - 1) * scale
    low, mid, high = mask * low, mask * scale, mask * high
    return lambda p: low if p < first else mid if p < last else high


def loop(first, last, body):
    for i in range(first, last):
        body(i)


def halving(rows, cols):
    a = lax.broadcasted_iota(jnp.int32, (rows, cols), 0)
    b = lax.broadcasted_iota(jnp.int32, (rows, cols), 1)
    return flag(a // 2 == b)


def doubling(rows, cols):
    a = lax.broadcasted_iota(jnp.int32, (rows, cols), 0)
    b = lax.broadcasted_iota(jnp.int32, (rows, cols), 1)
    return flag(b // 2 == a)


def dot(a, b):
    b = b.astype(jnp.bfloat16)
    hi = a.astype(jnp.bfloat16)
    a = a - hi.astype(F32)
    mid = a.astype(jnp.bfloat16)
    lo = (a - mid.astype(F32)).astype(jnp.bfloat16)
    one = functools.partial(jnp.dot, preferred_element_type=F32)
    return one(hi, b) + one(mid, b) + one(lo, b)


def turn(tile, by):
    by = by % 128
    return pltpu.roll(tile, by, 1) if by else tile


def x_plane(own, xlo, xhi, p):
    if p < HX:
        return xlo(p)
    return own(p - HX) if p < HX + BX else xhi(p - HX - BX)


def half_tile(src, base, plane):
    at = 4 * (plane % 2)
    return src[base + plane // 2, at : at + 4]


def first_parts(a, own, xlo, xhi, zl, zr, ylo, yhi):
    base = a * 84

    def parts(p):
        g, k = p // 5, p % 5

        def pair(center, left, right):
            lane = lax.broadcasted_iota(jnp.int32, left.shape, 1)
            return center, jnp.where(lane < 64, turn(right, -24 * k), turn(left, 104 - 24 * k))

        whole = lambda y: pair(y[base + p], y[base + 40 + g], y[base + 48 + g])
        half = lambda y: pair(*(half_tile(y, base + 56, m) for m in (p, 40 + g, 48 + g)))
        center = x_plane(lambda i: own[i], lambda i: xlo[a, i], lambda i: xhi[a, i], p)
        if ylo is None:
            return [((12, 44), None, pair(center, zl[a, g], zr[a, g]))]
        return list(zip(ROWS, SIDES, (whole(ylo), half(ylo), half(yhi), whole(yhi))))

    return parts


def later_parts(own, halo, xlo, xhi, ylo, yhi):
    def parts(p):
        g, k = p // 4, p % 4
        pair = lambda center, side: (center, turn(side, 112 - 32 * k))
        whole = lambda y: pair(y[p], y[40 + g])
        half = lambda y: pair(half_tile(y, 50, p), half_tile(y, 50, 40 + g))
        center = x_plane(lambda i: own[i], lambda i: xlo[i], lambda i: xhi[i], p)
        side = x_plane(
            lambda i: halo[i // 4], lambda i: xlo[12 + i // 4], lambda i: xhi[12 + i // 4], p
        )
        if ylo is None:
            return [((12, 44), None, pair(center, side))]
        return list(zip(ROWS, SIDES, (whole(ylo), half(ylo), half(yhi), whole(yhi))))

    return parts


ROWS, SIDES = ((0, 8), (8, 12), (44, 48), (48, 56)), (0, 0, 1, 1)


def assemble_field(dst, parts):
    gx, gy, gz = places()
    lane = lax.broadcasted_iota(jnp.int32, (1, BZ), 1)
    side = jnp.where(lane < 64, flag(gz < GZ - 1), flag(gz > 0))
    x_low, x_high = flag(gx > 0), flag(gx < GX - 1)
    y_sides = flag(gy > 0), flag(gy < GY - 1)
    for p in range(EX):
        x = x_low if p < HX else None if p < HX + BX else x_high
        for (lo, hi), y, (center, halo) in parts(p):
            y = None if y is None else y_sides[y]
            scale = x if y is None else y if x is None else x * y
            dst[p, lo:hi, :BZ] = center if scale is None else center * scale
            dst[p, lo:hi, BZ:] = halo * (side if scale is None else side * scale)


def assemble_diagonal(dst, parts):
    for p in range(EX):
        for (lo, hi), _, (center, halo) in parts(p):
            dst[p, lo:hi, :BZ] = center + 27.0
            dst[p, lo:hi, BZ:] = halo + 27.0


def z_pack_kernel(right_side, diagonal, xlo, xhi, down, up):
    group = lax.broadcasted_iota(jnp.int32, (BY, BZ), 1) // 24
    for a, own in enumerate((right_side, diagonal)):
        for g in range(EX // 5):
            low = high = None
            for k in range(5):
                src = x_plane(
                    lambda i: own[i], lambda i: xlo[a, i], lambda i: xhi[a, i], 5 * g + k
                )
                first, last = turn(src, 24 * k), turn(src, 24 * k - 104)
                low = first if k == 0 else jnp.where(group == k, first, low)
                high = last if k == 0 else jnp.where(group == k, last, high)
            down[a, g] = low
            up[a, g] = high


def y_rows(planes, base, down, up):
    count = len(planes)
    for m, plane in enumerate(planes):
        down[base + m] = plane(4, 12)
        up[base + m] = plane(20, 28)
        at = base + count + m // 2
        row = 4 * (m % 2)
        down[at, row : row + 4] = plane(0, 4)
        up[at, row : row + 4] = plane(28, 32)


def y_pack_kernel(right_side, diagonal, xlo, xhi, zl, zr, down, up):
    def rows(ref, *index):
        return lambda lo, hi: ref[(*index, slice(lo, hi))]

    for a, own in enumerate((right_side, diagonal)):
        planes = [
            x_plane(
                lambda i: rows(own, i), lambda i: rows(xlo, a, i), lambda i: rows(xhi, a, i), p
            )
            for p in range(EX)
        ]
        planes += [rows(zl, a, g) for g in range(8)] + [rows(zr, a, g) for g in range(8)]
        y_rows(planes, 84 * a, down, up)


def y_pack_later_kernel(own, halo, xlo, xhi, down, up):
    def rows(ref, index):
        return lambda lo, hi: ref[index, lo:hi]

    planes = [
        x_plane(lambda i: rows(own, i), lambda i: rows(xlo, i), lambda i: rows(xhi, i), p)
        for p in range(EX)
    ]
    planes += [
        x_plane(
            lambda i: rows(halo, i // 4),
            lambda i: rows(xlo, 12 + i // 4),
            lambda i: rows(xhi, 12 + i // 4),
            4 * g,
        )
        for g in range(10)
    ]
    y_rows(planes, 0, down, up)


def halve(pairs, rows, z_map, dst, scale):
    rows[...] = dot(pairs[...], z_map)
    for p in range(MX):
        at = p * EY
        total = rows[pl.ds(at, MR, stride=2), :] + rows[pl.ds(at + 1, MR, stride=2), :]
        dst[p, :MR] = total * scale
        dst[p, MR:] = jnp.zeros((MY - MR, MZ), F32)


def early_kernel(first, *refs):
    if first:
        right_side, diagonal, xlo, xhi, zl, zr, field, zfull, d0 = refs
        assemble_field(field, first_parts(0, right_side, xlo, xhi, zl, zr, None, None))
        assemble_diagonal(d0, first_parts(1, diagonal, xlo, xhi, zl, zr, None, None))
    else:
        own, halo, xlo, xhi, d0, field, zfull = refs
        assemble_field(field, later_parts(own, halo, xlo, xhi, None, None))
    mask = x_masks(plane_mask(0, (24, EZ), 16 - HY), 0, CA)
    for p in range(1, EX - 1):
        total = field[p - 1, 8:48] + field[p, 8:48] + field[p + 1, 8:48]
        box = spread_z(spread_y(total)[8:32])
        zfull[p, 16:40] = (CR + CA * d0[p, 16:40]) * field[p, 16:40] - mask(p) * box


def pre_kernel(first, *refs):
    if first:
        right_side, diagonal, xlo, xhi, zl, zr, ylo, yhi = refs[:8]
        field, zfull, d0, d1, zs, rs, z1, left1, packed, pairs, rows, r1, small = refs[11:]
        assemble_field(field, first_parts(0, right_side, xlo, xhi, zl, zr, ylo, yhi))
    else:
        own, halo, xlo, xhi, ylo, yhi = refs[:6]
        d0, d1 = refs[8:10]
        field, zfull, zs, rs, z1, left1, packed, pairs, rows, r1, small = refs[10:]
        assemble_field(field, later_parts(own, halo, xlo, xhi, ylo, yhi))
    z_map = halving(EZ, MZ)
    if first:
        assemble_diagonal(d0, first_parts(1, diagonal, xlo, xhi, zl, zr, ylo, yhi))
        for i in range(MX):
            pairs[i * EY : (i + 1) * EY, :] = d0[2 * i] + d0[2 * i + 1]
        halve(pairs, rows, z_map, d1, 0.125)
    pairs[0:EY, :] = jnp.zeros((EY, EZ), F32)
    pairs[(MX - 1) * EY :, :] = jnp.zeros((EY, EZ), F32)
    low = x_masks(plane_mask(0, (16, EZ), -HY), 0, CA)
    high = x_masks(plane_mask(0, (16, EZ), 40 - HY), 0, CA)

    def smooth(p):
        total = field[p - 1, 0:24] + field[p, 0:24] + field[p + 1, 0:24]
        box = spread_z(spread_y(total)[0:16])
        zfull[p, 0:16] = (CR + CA * d0[p, 0:16]) * field[p, 0:16] - low(p) * box
        total = field[p - 1, 32:56] + field[p, 32:56] + field[p + 1, 32:56]
        box = spread_z(spread_y(total)[8:24])
        zfull[p, 40:56] = (CR + CA * d0[p, 40:56]) * field[p, 40:56] - high(p) * box
        if 10 <= p < 30:
            zs[p - 10] = zfull[p, 8:48]

    def rest(p):
        z = zfull[p]
        left = field[p] - d0[p] * z + spread(zfull[p - 1] + z + zfull[p + 1])
        if 10 <= p < 30:
            rs[p - 10] = left[8:48]
        return left

    def rest_pair(i):
        pairs[i * EY : (i + 1) * EY, :] = rest(2 * i) + rest(2 * i + 1)

    loop(1, EX - 1, smooth)
    loop(1, MX - 1, rest_pair)
    halve(pairs, rows, z_map, r1, 0.5)
    mask1 = plane_mask(1, (MY, MZ), -HY // 2)
    keep1, mask1 = x_masks(mask1, 1), x_masks(mask1, 1, CA)

    def mask_one(p):
        r1[p] = r1[p] * keep1(p)

    loop(0, MX, mask_one)

    def smooth_one(p):
        r = r1[p]
        box = spread(r1[p - 1] + r + r1[p + 1])
        z1[p] = (CR + CA * d1[p]) * r - mask1(p) * box

    zero = jnp.zeros((MY, MZ), F32)
    for ref in (z1, left1):
        ref[0] = zero
        ref[MX - 1] = zero
    loop(1, MX - 1, smooth_one)

    def rest_one(p):
        z = z1[p]
        left1[p] = r1[p] - d1[p] * z + spread(z1[p - 1] + z + z1[p + 1])

    loop(1, MX - 1, rest_one)

    lane = lax.broadcasted_iota(jnp.int32, (MZ, 128), 0)
    col = lax.broadcasted_iota(jnp.int32, (MZ, 128), 1)

    def pack(src, scale):
        total = jnp.zeros((16, 128), F32)
        for k in range(4):
            s = src[6 + 2 * k, 6:22, :] + src[7 + 2 * k, 6:22, :]
            total = total + dot(s, flag((lane // 2 + 32 * k == col) & (lane < 64)))
        small[...] = total
        return (small[pl.ds(0, 8, stride=2), :] + small[pl.ds(1, 8, stride=2), :]) * scale

    tile = pack(left1, 0.5)
    if first:
        tile = jnp.concatenate([tile, pack(d1, 0.125)], axis=0)
    for i in range(GX * GZ):
        packed[i] = tile


def unpack(dst, row, lo, own, hi, scales):
    group = lax.broadcasted_iota(jnp.int32, (8, 128), 1) // 32
    for part, (src, scale) in enumerate(zip((lo, own, hi), scales)):
        for bx in range(GX):
            for k in range(4):
                for h in range(2):
                    acc = None
                    for j in range(4):
                        block = turn(src[bx * GZ + 4 * h + j, row : row + 8, :], 32 * (j - k))
                        acc = block if acc is None else jnp.where(group == j, block, acc)
                    rows = slice(8 * part, 8 * part + 8)
                    lanes = slice(128 * h, 128 * h + 128)
                    dst[6 + 4 * bx + k, rows, lanes] = acc if scale is None else acc * scale
    for p in (*range(6), *range(22, 28)):
        dst[p] = jnp.zeros((24, 256), F32)


def coarse(r2, d2, s0, s1, z2):
    gx, gy, _ = places()
    shape = (24, 256)
    row = lax.broadcasted_iota(jnp.int32, shape, 0) + (gy * 8 - 8)
    mask = flag((row >= 0) & (row < 64))
    low, high = mask * flag(gx > 0), mask * flag(gx < GX - 1)
    inside = lambda i: low if i < 6 else mask if i < 10 else high
    lane = lax.broadcasted_iota(jnp.int32, shape, 1)
    at = lambda ref, i: ref[4 * gx + i]

    def box(t):
        t = t + pltpu.roll(t, 1, 0) + pltpu.roll(t, 23, 0)
        return (
            t
            + jnp.where(lane == 0, 0.0, pltpu.roll(t, 1, 1))
            + jnp.where(lane == 255, 0.0, pltpu.roll(t, 255, 1))
        )

    theta, delta = 29.5, 28.5
    sigma = theta / delta
    rho = 1.0 / sigma
    rho1 = 1.0 / (2.0 * sigma - rho)
    rho2 = 1.0 / (2.0 * sigma - rho1)

    for i in range(2, 14):
        r = at(r2, i)
        step = r * (1.0 / theta)
        total = box(at(r2, i - 1) + r + at(r2, i + 1)) * (1.0 / theta)
        remain = inside(i) * (r - at(d2, i) * step + total)
        s0[i] = remain
        s1[i] = (rho1 * rho) * step + (2.0 * rho1 / delta) * remain
    for i in range(3, 13):
        step = s1[i]
        remain = inside(i) * (s0[i] - at(d2, i) * step + box(s1[i - 1] + step + s1[i + 1]))
        last = (rho2 * rho1) * step + (2.0 * rho2 / delta) * remain
        z2[i] = at(r2, i) * (1.0 / theta) + step + last
    for i in range(4, 12):
        y, d = z2[i], at(d2, i)
        left = at(r2, i) - d * y + box(z2[i - 1] + y + z2[i + 1])
        top = jnp.sum(left, axis=1, keepdims=True)
        bottom = jnp.sum(d - 26.0, axis=1, keepdims=True)
        s0[i] = inside(i) * (y + top / bottom)


def post_kernel(first, *refs):
    lo, own, hi, zs, rs, z1, left1, d0, d1 = refs[:9]
    if first:
        d2, z_core, q_core, q_down, q_up, q_halo = refs[9:15]
    else:
        d2, r_old, z_old, q_old, z_core, q_core, dots = refs[9:16]
    r2, s0, s1, z2, wide, rows1, u, rem, zf1, rowsv, v, sv, rem0, zf0 = refs[-14:]
    gx, gy, gz = places()
    scales = (flag(gy > 0), None, flag(gy < GY - 1))
    unpack(r2, 0, lo, own, hi, scales)
    if first:
        unpack(d2, 8, lo, own, hi, (None, None, None))
    coarse(r2, d2, s0, s1, z2)

    lane = lax.broadcasted_iota(jnp.int32, (16, 128), 1)
    z = jnp.where(lane < 48, lane, lane - 64) + 32 * gz
    in2 = flag((z >= 0) & (z < 256) & (lane < 64))
    turned = (256 - 32 * gz) % 256
    for i in range(8):
        plane = pltpu.roll(s0[i + 4], turned, 1)[5:21]
        plane = jnp.where(lane < 48, plane[:, :128], turn(plane[:, 128:], 64))
        wide[16 * i : 16 * i + 16, :] = plane * in2
    up = dot(wide[...], doubling(128, 128))
    rows1[pl.ds(0, 128, stride=2), :] = up
    rows1[pl.ds(1, 128, stride=2), :] = up
    u[1:9] = rows1[...].reshape(8, 32, 128)

    mask1 = plane_mask(1, (MY, MZ), -HY // 2)
    keep1, mask1 = x_masks(mask1, 1), x_masks(mask1, 1, CA)

    def remain_one(p):
        c = u[p // 2]
        total = u[(p - 1) // 2] + c + u[(p + 1) // 2]
        rem[p] = keep1(p) * (left1[p] - d1[p] * c + spread(total))

    loop(3, 17, remain_one)

    def final_one(p):
        r = rem[p]
        box = spread(rem[p - 1] + r + rem[p + 1])
        f = z1[p] + u[p // 2] + ((CR + CA * d1[p]) * r - mask1(p) * box)
        zf1[(p - 4) * 20 : (p - 3) * 20, :] = f[4:24]

    loop(4, 16, final_one)

    rowsv[pl.ds(0, 240, stride=2), :] = zf1[...]
    rowsv[pl.ds(1, 240, stride=2), :] = zf1[...]
    v[...] = dot(rowsv[...], doubling(128, 256)).reshape(12, PY, EZ)
    for i in range(12):
        sv[i] = spread(v[i])

    mask0 = plane_mask(0, (PY, EZ), -4)
    keep0, mask0 = x_masks(mask0, 0), x_masks(mask0, 0, CA)

    def remain(i):
        p = i + 10
        at = p // 2 - 4
        other = (p - 1) // 2 - 4 if p % 2 == 0 else (p + 1) // 2 - 4
        rem0[i] = keep0(p) * (rs[i] - d0[p, 8:48, :] * v[at] + (2.0 * sv[at] + sv[other]))

    loop(0, 20, remain)

    def final(i):
        p = i + 10
        r = rem0[i]
        box = spread(rem0[i - 1] + r + rem0[i + 1])
        zf0[i] = zs[i] + v[p // 2 - 4] + ((CR + CA * d0[p, 8:48, :]) * r - mask0(p) * box)

    loop(1, 19, final)

    group = lax.broadcasted_iota(jnp.int32, (BY, BZ), 1) // 32
    acc = [None] * 9

    def apply(i):
        c = zf0[i + 2]
        q = d0[i + HX, 8:48, :] * c - spread(zf0[i + 1] + c + zf0[i + 3])
        q_own, z_own = q[4:36, :BZ], c[4:36, :BZ]
        z_core[i] = z_own
        q_core[i] = q_own
        if not first:
            for k, term in enumerate(products(r_old[i], z_old[i], q_old[i], z_own, q_own)):
                term = term[:8] + term[8:16] + (term[16:24] + term[24:])
                acc[k] = term if i == 0 else acc[k] + term
        if first:
            if i < 12:
                q_down[i] = q_own
            if i >= 4:
                q_up[i - 4] = q_own
            g, k = i // 4, i % 4
            halo = turn(q[4:36, BZ:], 32 * k - 112)
            if k:
                halo = jnp.where(group == k, halo, q_halo[g])
            q_halo[g] = halo
            if k == 3 and g < 3:
                q_down[12 + g] = halo
            if k == 3 and g > 0:
                q_up[11 + g] = halo

    loop(0, BX, apply)
    if not first:
        lane = lax.broadcasted_iota(jnp.int32, (1, 128), 1)
        row = jnp.zeros((1, 128), F32)
        for k, part in enumerate(acc):
            total = jnp.sum(jnp.sum(part, axis=0, keepdims=True), axis=1, keepdims=True)
            row = jnp.where(lane == k, total, row)
        dots[...] = jnp.broadcast_to(row[None], dots.shape)


def products(r, z, q, p, w):
    r1, z1, w1 = r - q, z - p, q - w
    return (
        r * z, z * q, r1 * z1, r1 * p + q * z1, q * p, z1 * w1, z1 * w + p * w1, p * w, z1 * q,
    )


def end_kernel(r, z, q, p, w, sums, solution_field, residual):
    last = jnp.sum(sums[...], axis=0)
    lane = lax.broadcasted_iota(jnp.int32, (1, 128), 1)
    at = lambda i: jnp.sum(jnp.where(lane == i, last, 0.0), axis=1, keepdims=True)
    rz, curve = at(0), at(1)
    alpha = rz / curve
    t = alpha - 1.0
    rz2 = at(2) - t * at(3) + t * t * at(4)
    zw = at(5) - t * at(6) + t * t * at(7)
    zq = at(8) - t * at(4)
    beta = rz2 / rz
    alpha2 = rz2 / (zw + 2.0 * beta * zq + beta * beta * curve)

    def body(i):
        zi, qi = z[i], q[i]
        solution_field[i] = alpha * zi + alpha2 * ((zi - alpha * p[i]) + beta * zi)
        residual[i] = (r[i] - alpha * qi) - alpha2 * ((qi - alpha * w[i]) + beta * qi)

    loop(0, BX, body)


def shape(*dims):
    return jax.ShapeDtypeStruct(dims, F32)


def call(kernel, outs, scratch, *args, aliases=None):
    whole = pl.BlockSpec(memory_space=pltpu.VMEM)
    return pl.pallas_call(
        kernel,
        out_shape=outs,
        in_specs=[whole] * len(args),
        out_specs=jax.tree.map(lambda _: whole, outs),
        scratch_shapes=[pltpu.VMEM(s, F32) for s in scratch],
        input_output_aliases=aliases or {},
        compiler_params=pltpu.CompilerParams(vmem_limit_bytes=24 * 1024 * 1024),
    )(*args)


def shift(value, axis, count, by):
    return lax.ppermute(value, axis, [(i, (i + by) % count) for i in range(count)])


def spread_coarse(packed):
    own = lax.all_to_all(packed, ("gx", "gz"), 0, 0)
    return shift(own, "gy", GY, 1), own, shift(own, "gy", GY, -1)


def early_call(first, *args):
    big = shape(EX, EY, EZ)
    return call(functools.partial(early_kernel, first), (big,) * (3 if first else 2), [], *args)


def pre_call(first, pieces, early, given=()):
    big = shape(EX, EY, EZ)
    kept = (shape(20, PY, EZ), shape(20, PY, EZ), shape(MX, MY, MZ), shape(MX, MY, MZ),
            shape(GX * GZ, 16 if first else 8, 128))
    scratch = [(MX * EY, EZ), (MX * EY, MZ), (MX, MY, MZ), (16, 128)]
    outs = (big,) * len(early) + ((shape(MX, MY, MZ),) if first else ()) + kept
    aliases = {len(pieces) + i: i for i in range(len(early))}
    kernel = functools.partial(pre_kernel, first)
    return call(kernel, outs, scratch, *pieces, *early, *given, aliases=aliases)[2:]


def post_call(parts, kept, d0, d1, *old):
    first = not old
    scratch = [(28, 24, 256)] + [(16, 24, 256)] * 3 + [
        (128, 128), (256, 128), (10, 32, 128), (MX, MY, MZ), (240, 128),
        (480, 128), (12, PY, EZ), (12, PY, EZ), (20, PY, EZ), (20, PY, EZ),
    ]
    core = shape(BX, BY, BZ)
    kernel = functools.partial(post_kernel, first)
    if first:
        slab = shape(15, BY, BZ)
        outs = (shape(28, 24, 256), core, core, slab, slab, shape(4, BY, BZ))
        return call(kernel, outs, scratch, *parts, *kept, d0, d1)
    outs = (core, core, shape(GX * GY * GZ, 1, 128))
    return call(kernel, outs, scratch, *parts, *kept, d0, d1, *old)


def first_exchange(right_side, diagonal):
    def slab(lo, hi):
        return jnp.stack([right_side[lo:hi], diagonal[lo:hi]])

    xlo = shift(slab(BX - HX, BX), "gx", GX, 1)
    xhi = shift(slab(0, HX), "gx", GX, -1)
    edge = shape(2, EX // 5, BY, BZ)
    down, up = call(z_pack_kernel, (edge, edge), [], right_side, diagonal, xlo, xhi)
    zl = shift(up, "gz", GZ, 1)
    zr = shift(down, "gz", GZ, -1)
    edge = shape(168, 8, BZ)
    pieces = (right_side, diagonal, xlo, xhi, zl, zr)
    down, up = call(y_pack_kernel, (edge, edge), [], *pieces)
    early = early_call(True, *pieces)
    return (*pieces, shift(up, "gy", GY, 1), shift(down, "gy", GY, -1)), early


def later_exchange(d0, q, q_down, q_up, q_halo):
    xlo = shift(q_up, "gx", GX, 1)
    xhi = shift(q_down, "gx", GX, -1)
    edge = shape(75, 8, BZ)
    down, up = call(y_pack_later_kernel, (edge, edge), [], q, q_halo, xlo, xhi)
    early = early_call(False, q, q_halo, xlo, xhi, d0)
    return (q, q_halo, xlo, xhi, shift(up, "gy", GY, 1), shift(down, "gy", GY, -1)), early


def local(right_side, diagonal):
    d0, d1, *kept = pre_call(True, *first_exchange(right_side, diagonal))
    d2, z, q, *edges = post_call(spread_coarse(kept[-1]), kept[:-1], d0, d1)
    kept = pre_call(False, *later_exchange(d0, q, *edges), (d0, d1))
    p, w, dots = post_call(
        spread_coarse(kept[-1]), kept[:-1], d0, d1, d2, right_side, z, q
    )
    sums = lax.all_to_all(dots, ("gx", "gy", "gz"), 0, 0)
    core = shape(BX, BY, BZ)
    return call(end_kernel, (core, core), [], right_side, z, q, p, w, sums)


def solution(mesh):
    return jax.shard_map(
        local, mesh=mesh, in_specs=(SPEC, SPEC), out_specs=(SPEC, SPEC), check_vma=False
    )
```

```python
import functools

import jax
import jax.numpy as jnp
from jax import lax
from jax.experimental import pallas as pl
from jax.experimental.pallas import tpu as pltpu
from jax.sharding import PartitionSpec as P

GX, GY, GZ = 4, 8, 8
BX, BY, BZ = 16, 32, 128
HX, HY = 12, 12
EX, EY, EZ = BX + 2 * HX, BY + 2 * HY, 2 * BZ
MX, MR, MY, MZ = EX // 2, EY // 2, 32, BZ
PY = BY + 8
F32 = jnp.float32
SPEC = P("gx", "gy", "gz")


def cheb_two(lower, upper=58.0):
    theta, delta = (upper + lower) / 2.0, (upper - lower) / 2.0
    sigma = theta / delta
    rho = 1.0 / sigma
    after = 1.0 / (2.0 * sigma - rho)
    return (1.0 + after * rho) / theta + 2.0 * after / delta, -2.0 * after / (delta * theta)


CR, CA = cheb_two(7.0)


def spread_y(t):
    return t + pltpu.roll(t, 1, 0) + pltpu.roll(t, t.shape[0] - 1, 0)


def spread_z(t):
    return t + pltpu.roll(t, 1, 1) + pltpu.roll(t, t.shape[1] - 1, 1)


def spread(t):
    return spread_z(spread_y(t))


def flag(condition):
    return jnp.where(condition, 1.0, 0.0).astype(F32)


def places():
    return lax.axis_index("gx"), lax.axis_index("gy"), lax.axis_index("gz")


def plane_mask(level, shape, row):
    _, gy, gz = places()
    size = 1 << level
    y = lax.broadcasted_iota(jnp.int32, shape, 0) + (gy * (BY // size) + row)
    lane = lax.broadcasted_iota(jnp.int32, shape, 1)
    z = jnp.where(lane < 3 * shape[1] // 4, lane, lane - shape[1]) + gz * (BZ // size)
    return flag((y >= 0) & (y < GY * BY // size) & (z >= 0) & (z < GZ * BZ // size))


def x_masks(mask, level, scale=1.0):
    gx = places()[0]
    first, last = HX >> level, (HX + BX) >> level
    low, high = flag(gx > 0) * scale, flag(gx < GX - 1) * scale
    low, mid, high = mask * low, mask * scale, mask * high
    return lambda p: low if p < first else mid if p < last else high


def loop(first, last, body):
    for i in range(first, last):
        body(i)


def halving(rows, cols):
    a = lax.broadcasted_iota(jnp.int32, (rows, cols), 0)
    b = lax.broadcasted_iota(jnp.int32, (rows, cols), 1)
    return flag(a // 2 == b)


def doubling(rows, cols):
    a = lax.broadcasted_iota(jnp.int32, (rows, cols), 0)
    b = lax.broadcasted_iota(jnp.int32, (rows, cols), 1)
    return flag(b // 2 == a)


def dot(a, b):
    b = b.astype(jnp.bfloat16)
    hi = a.astype(jnp.bfloat16)
    a = a - hi.astype(F32)
    mid = a.astype(jnp.bfloat16)
    lo = (a - mid.astype(F32)).astype(jnp.bfloat16)
    one = functools.partial(jnp.dot, preferred_element_type=F32)
    return one(hi, b) + one(mid, b) + one(lo, b)


def turn(tile, by):
    by = by % 128
    return pltpu.roll(tile, by, 1) if by else tile


def x_plane(own, xlo, xhi, p):
    if p < HX:
        return xlo(p)
    return own(p - HX) if p < HX + BX else xhi(p - HX - BX)


def half_tile(src, base, plane):
    at = 4 * (plane % 2)
    return src[base + plane // 2, at : at + 4]


def first_parts(a, own, xlo, xhi, zl, zr, ylo, yhi):
    base = a * 84

    def parts(p):
        g, k = p // 5, p % 5

        def pair(center, left, right):
            lane = lax.broadcasted_iota(jnp.int32, left.shape, 1)
            return center, jnp.where(lane < 64, turn(right, -24 * k), turn(left, 104 - 24 * k))

        whole = lambda y: pair(y[base + p], y[base + 40 + g], y[base + 48 + g])
        half = lambda y: pair(*(half_tile(y, base + 56, m) for m in (p, 40 + g, 48 + g)))
        center = x_plane(lambda i: own[i], lambda i: xlo[a, i], lambda i: xhi[a, i], p)
        if ylo is None:
            return [((12, 44), None, pair(center, zl[a, g], zr[a, g]))]
        return list(zip(ROWS, SIDES, (whole(ylo), half(ylo), half(yhi), whole(yhi))))

    return parts


def later_parts(own, halo, xlo, xhi, ylo, yhi):
    def parts(p):
        g, k = p // 4, p % 4
        pair = lambda center, side: (center, turn(side, 112 - 32 * k))
        whole = lambda y: pair(y[p], y[40 + g])
        half = lambda y: pair(half_tile(y, 50, p), half_tile(y, 50, 40 + g))
        center = x_plane(lambda i: own[i], lambda i: xlo[i], lambda i: xhi[i], p)
        side = x_plane(
            lambda i: halo[i // 4], lambda i: xlo[12 + i // 4], lambda i: xhi[12 + i // 4], p
        )
        if ylo is None:
            return [((12, 44), None, pair(center, side))]
        return list(zip(ROWS, SIDES, (whole(ylo), half(ylo), half(yhi), whole(yhi))))

    return parts


ROWS, SIDES = ((0, 8), (8, 12), (44, 48), (48, 56)), (0, 0, 1, 1)


def assemble_field(dst, parts):
    gx, gy, gz = places()
    lane = lax.broadcasted_iota(jnp.int32, (1, BZ), 1)
    side = jnp.where(lane < 64, flag(gz < GZ - 1), flag(gz > 0))
    x_low, x_high = flag(gx > 0), flag(gx < GX - 1)
    y_sides = flag(gy > 0), flag(gy < GY - 1)
    for p in range(EX):
        x = x_low if p < HX else None if p < HX + BX else x_high
        for (lo, hi), y, (center, halo) in parts(p):
            y = None if y is None else y_sides[y]
            scale = x if y is None else y if x is None else x * y
            dst[p, lo:hi, :BZ] = center if scale is None else center * scale
            dst[p, lo:hi, BZ:] = halo * (side if scale is None else side * scale)


def assemble_diagonal(dst, parts):
    for p in range(EX):
        for (lo, hi), _, (center, halo) in parts(p):
            dst[p, lo:hi, :BZ] = center + 27.0
            dst[p, lo:hi, BZ:] = halo + 27.0


def z_pack_kernel(right_side, diagonal, xlo, xhi, down, up):
    group = lax.broadcasted_iota(jnp.int32, (BY, BZ), 1) // 24
    for a, own in enumerate((right_side, diagonal)):
        for g in range(EX // 5):
            low = high = None
            for k in range(5):
                src = x_plane(
                    lambda i: own[i], lambda i: xlo[a, i], lambda i: xhi[a, i], 5 * g + k
                )
                first, last = turn(src, 24 * k), turn(src, 24 * k - 104)
                low = first if k == 0 else jnp.where(group == k, first, low)
                high = last if k == 0 else jnp.where(group == k, last, high)
            down[a, g] = low
            up[a, g] = high


def y_rows(planes, base, down, up):
    count = len(planes)
    for m, plane in enumerate(planes):
        down[base + m] = plane(4, 12)
        up[base + m] = plane(20, 28)
        at = base + count + m // 2
        row = 4 * (m % 2)
        down[at, row : row + 4] = plane(0, 4)
        up[at, row : row + 4] = plane(28, 32)


def y_pack_kernel(right_side, diagonal, xlo, xhi, zl, zr, down, up):
    def rows(ref, *index):
        return lambda lo, hi: ref[(*index, slice(lo, hi))]

    for a, own in enumerate((right_side, diagonal)):
        planes = [
            x_plane(
                lambda i: rows(own, i), lambda i: rows(xlo, a, i), lambda i: rows(xhi, a, i), p
            )
            for p in range(EX)
        ]
        planes += [rows(zl, a, g) for g in range(8)] + [rows(zr, a, g) for g in range(8)]
        y_rows(planes, 84 * a, down, up)


def y_pack_later_kernel(own, halo, xlo, xhi, down, up):
    def rows(ref, index):
        return lambda lo, hi: ref[index, lo:hi]

    planes = [
        x_plane(lambda i: rows(own, i), lambda i: rows(xlo, i), lambda i: rows(xhi, i), p)
        for p in range(EX)
    ]
    planes += [
        x_plane(
            lambda i: rows(halo, i // 4),
            lambda i: rows(xlo, 12 + i // 4),
            lambda i: rows(xhi, 12 + i // 4),
            4 * g,
        )
        for g in range(10)
    ]
    y_rows(planes, 0, down, up)


def z_halve(rows, pairs, chunks):
    size = sum(hi - lo for lo, hi in chunks)
    narrow = dot(pairs[...], halving(EZ, MZ))
    for i in range(MX):
        at = i * size
        for lo, hi in chunks:
            rows[i * EY + lo : i * EY + hi] = narrow[at : at + hi - lo]
            at += hi - lo


def y_halve(rows, dst, scale):
    for p in range(MX):
        at = p * EY
        total = rows[pl.ds(at, MR, stride=2), :] + rows[pl.ds(at + 1, MR, stride=2), :]
        dst[p, :MR] = total * scale
        dst[p, MR:] = jnp.zeros((MY - MR, MZ), F32)


def clear_ends(pairs):
    size = pairs.shape[0] // MX
    pairs[0:size] = jnp.zeros((size, EZ), F32)
    pairs[(MX - 1) * size :] = jnp.zeros((size, EZ), F32)


MIDDLE, OUTER = ((16, 40),), ((0, 16), (40, 56))


def early_kernel(first, *refs):
    if first:
        right_side, diagonal, xlo, xhi, zl, zr = refs[:6]
        field, zfull, zs, rs, rows, d0, d_rows, pairs = refs[6:]
        assemble_field(field, first_parts(0, right_side, xlo, xhi, zl, zr, None, None))
        assemble_diagonal(d0, first_parts(1, diagonal, xlo, xhi, zl, zr, None, None))
        for i in range(MX):
            pairs[24 * i : 24 * i + 24] = d0[2 * i, 16:40] + d0[2 * i + 1, 16:40]
        z_halve(d_rows, pairs, MIDDLE)
    else:
        own, halo, xlo, xhi, d0 = refs[:5]
        field, zfull, zs, rs, rows, pairs = refs[5:]
        assemble_field(field, later_parts(own, halo, xlo, xhi, None, None))
    mask = x_masks(plane_mask(0, (PY, EZ), 8 - HY), 0, CA)
    for p in range(1, EX - 1):
        r = field[p, 8:48]
        box = spread(field[p - 1, 8:48] + r + field[p + 1, 8:48])
        z = (CR + CA * d0[p, 8:48]) * r - mask(p) * box
        zfull[p, 8:48] = z
        if 10 <= p < 30:
            zs[p - 10, 8:32] = z[8:32]

    def rest(p):
        total = zfull[p - 1, 8:48] + zfull[p, 8:48] + zfull[p + 1, 8:48]
        box = spread_z(spread_y(total)[8:32])
        left = field[p, 16:40] - d0[p, 16:40] * zfull[p, 16:40] + box
        if 10 <= p < 30:
            rs[p - 10, 8:32] = left
        return left

    clear_ends(pairs)
    for i in range(1, MX - 1):
        pairs[24 * i : 24 * i + 24] = rest(2 * i) + rest(2 * i + 1)
    z_halve(rows, pairs, MIDDLE)


def pre_kernel(first, *refs):
    if first:
        right_side, diagonal, xlo, xhi, zl, zr, ylo, yhi = refs[:8]
        field, zfull, zs, rs, rows, d0, d_rows, d1 = refs[15:23]
        z1, left1, packed, pairs, r1, small = refs[23:]
        assemble_field(field, first_parts(0, right_side, xlo, xhi, zl, zr, ylo, yhi))
        assemble_diagonal(d0, first_parts(1, diagonal, xlo, xhi, zl, zr, ylo, yhi))
        for i in range(MX):
            at = 32 * i
            pairs[at : at + 16] = d0[2 * i, 0:16] + d0[2 * i + 1, 0:16]
            pairs[at + 16 : at + 32] = d0[2 * i, 40:56] + d0[2 * i + 1, 40:56]
        z_halve(d_rows, pairs, OUTER)
        y_halve(d_rows, d1, 0.125)
    else:
        own, halo, xlo, xhi, ylo, yhi = refs[:6]
        d0, d1 = refs[11:13]
        field, zfull, zs, rs, rows = refs[13:18]
        z1, left1, packed, pairs, r1, small = refs[18:]
        assemble_field(field, later_parts(own, halo, xlo, xhi, ylo, yhi))
    low = x_masks(plane_mask(0, (16, EZ), -HY), 0, CA)
    high = x_masks(plane_mask(0, (16, EZ), 40 - HY), 0, CA)

    def smooth(p):
        total = field[p - 1, 0:24] + field[p, 0:24] + field[p + 1, 0:24]
        box = spread_z(spread_y(total)[0:16])
        z = (CR + CA * d0[p, 0:16]) * field[p, 0:16] - low(p) * box
        zfull[p, 0:16] = z
        total = field[p - 1, 32:56] + field[p, 32:56] + field[p + 1, 32:56]
        box = spread_z(spread_y(total)[8:24])
        y = (CR + CA * d0[p, 40:56]) * field[p, 40:56] - high(p) * box
        zfull[p, 40:56] = y
        if 10 <= p < 30:
            zs[p - 10, 0:8] = z[8:16]
            zs[p - 10, 32:40] = y[0:8]

    def rest(p):
        total = zfull[p - 1, 0:24] + zfull[p, 0:24] + zfull[p + 1, 0:24]
        box = spread_z(spread_y(total)[0:16])
        a = field[p, 0:16] - d0[p, 0:16] * zfull[p, 0:16] + box
        total = zfull[p - 1, 32:56] + zfull[p, 32:56] + zfull[p + 1, 32:56]
        box = spread_z(spread_y(total)[8:24])
        b = field[p, 40:56] - d0[p, 40:56] * zfull[p, 40:56] + box
        if 10 <= p < 30:
            rs[p - 10, 0:8] = a[8:16]
            rs[p - 10, 32:40] = b[0:8]
        return a, b

    clear_ends(pairs)
    loop(1, EX - 1, smooth)
    for i in range(1, MX - 1):
        (a, b), (c, d) = rest(2 * i), rest(2 * i + 1)
        pairs[32 * i : 32 * i + 16] = a + c
        pairs[32 * i + 16 : 32 * i + 32] = b + d
    z_halve(rows, pairs, OUTER)
    y_halve(rows, r1, 0.5)
    mask1 = plane_mask(1, (MY, MZ), -HY // 2)
    keep1, mask1 = x_masks(mask1, 1), x_masks(mask1, 1, CA)

    def mask_one(p):
        r1[p] = r1[p] * keep1(p)

    loop(0, MX, mask_one)

    def smooth_one(p):
        r = r1[p]
        box = spread(r1[p - 1] + r + r1[p + 1])
        z1[p] = (CR + CA * d1[p]) * r - mask1(p) * box

    zero = jnp.zeros((MY, MZ), F32)
    for ref in (z1, left1):
        ref[0] = zero
        ref[MX - 1] = zero
    loop(1, MX - 1, smooth_one)

    def rest_one(p):
        z = z1[p]
        left1[p] = r1[p] - d1[p] * z + spread(z1[p - 1] + z + z1[p + 1])

    loop(1, MX - 1, rest_one)

    lane = lax.broadcasted_iota(jnp.int32, (MZ, 128), 0)
    col = lax.broadcasted_iota(jnp.int32, (MZ, 128), 1)

    def pack(src, scale):
        total = jnp.zeros((16, 128), F32)
        for k in range(4):
            s = src[6 + 2 * k, 6:22, :] + src[7 + 2 * k, 6:22, :]
            at = 32 * ((k + places()[2]) % 4)
            total = total + dot(s, flag((lane // 2 + at == col) & (lane < 64)))
        small[...] = total
        return (small[pl.ds(0, 8, stride=2), :] + small[pl.ds(1, 8, stride=2), :]) * scale

    tile = pack(left1, 0.5)
    if first:
        tile = jnp.concatenate([tile, pack(d1, 0.125)], axis=0)
    for i in range(GX * GZ):
        packed[i] = tile


def unpack(dst, row, lo, own, hi, scales):
    group = lax.broadcasted_iota(jnp.int32, (8, 128), 1) // 32
    for part, (src, scale) in enumerate(zip((lo, own, hi), scales)):
        for bx in range(GX):
            for k in range(4):
                for h in range(2):
                    acc = None
                    for j in range(4):
                        block = src[bx * GZ + 4 * h + j, row : row + 8, :]
                        here = group == (j + k) % 4
                        acc = block if acc is None else jnp.where(here, block, acc)
                    acc = turn(acc, -32 * k)
                    rows = slice(8 * part, 8 * part + 8)
                    lanes = slice(128 * h, 128 * h + 128)
                    dst[6 + 4 * bx + k, rows, lanes] = acc if scale is None else acc * scale
    for p in (*range(6), *range(22, 28)):
        dst[p] = jnp.zeros((24, 256), F32)


def coarse(r2, d2, s0, s1, z2):
    gx, gy, _ = places()
    shape = (24, 256)
    row = lax.broadcasted_iota(jnp.int32, shape, 0) + (gy * 8 - 8)
    mask = flag((row >= 0) & (row < 64))
    low, high = mask * flag(gx > 0), mask * flag(gx < GX - 1)
    inside = lambda i: low if i < 6 else mask if i < 10 else high
    lane = lax.broadcasted_iota(jnp.int32, shape, 1)
    at = lambda ref, i: ref[4 * gx + i]

    def box(t):
        t = t + pltpu.roll(t, 1, 0) + pltpu.roll(t, 23, 0)
        return (
            t
            + jnp.where(lane == 0, 0.0, pltpu.roll(t, 1, 1))
            + jnp.where(lane == 255, 0.0, pltpu.roll(t, 255, 1))
        )

    theta, delta = 29.5, 28.5
    sigma = theta / delta
    rho = 1.0 / sigma
    rho1 = 1.0 / (2.0 * sigma - rho)
    rho2 = 1.0 / (2.0 * sigma - rho1)

    for i in range(2, 14):
        r = at(r2, i)
        step = r * (1.0 / theta)
        total = box(at(r2, i - 1) + r + at(r2, i + 1)) * (1.0 / theta)
        remain = inside(i) * (r - at(d2, i) * step + total)
        s0[i] = remain
        s1[i] = (rho1 * rho) * step + (2.0 * rho1 / delta) * remain
    for i in range(3, 13):
        step = s1[i]
        remain = inside(i) * (s0[i] - at(d2, i) * step + box(s1[i - 1] + step + s1[i + 1]))
        last = (rho2 * rho1) * step + (2.0 * rho2 / delta) * remain
        z2[i] = at(r2, i) * (1.0 / theta) + step + last
    for i in range(4, 12):
        y, d = z2[i], at(d2, i)
        left = at(r2, i) - d * y + box(z2[i - 1] + y + z2[i + 1])
        top = jnp.sum(left, axis=1, keepdims=True)
        bottom = jnp.sum(d - 26.0, axis=1, keepdims=True)
        s0[i] = inside(i) * (y + top / bottom)


def post_kernel(first, *refs):
    lo, own, hi, zs, rs, z1, left1, d0, d1 = refs[:9]
    if first:
        d2, z_core, q_core, q_down, q_up, q_halo = refs[9:15]
    else:
        d2, r_old, z_old, q_old, z_core, q_core, dots = refs[9:16]
    r2, s0, s1, z2, wide, rows1, u, rem, zf1, rowsv, v, sv, rem0, zf0 = refs[-14:]
    gx, gy, gz = places()
    scales = (flag(gy > 0), None, flag(gy < GY - 1))
    unpack(r2, 0, lo, own, hi, scales)
    if first:
        unpack(d2, 8, lo, own, hi, (None, None, None))
    coarse(r2, d2, s0, s1, z2)

    lane = lax.broadcasted_iota(jnp.int32, (16, 128), 1)
    z = jnp.where(lane < 48, lane, lane - 64) + 32 * gz
    in2 = flag((z >= 0) & (z < 256) & (lane < 64))
    turned = (256 - 32 * gz) % 256
    for i in range(8):
        plane = pltpu.roll(s0[i + 4], turned, 1)[5:21]
        plane = jnp.where(lane < 48, plane[:, :128], turn(plane[:, 128:], 64))
        wide[16 * i : 16 * i + 16, :] = plane * in2
    up = dot(wide[...], doubling(128, 128))
    rows1[pl.ds(0, 128, stride=2), :] = up
    rows1[pl.ds(1, 128, stride=2), :] = up
    u[1:9] = rows1[...].reshape(8, 32, 128)

    mask1 = plane_mask(1, (MY, MZ), -HY // 2)
    keep1, mask1 = x_masks(mask1, 1), x_masks(mask1, 1, CA)

    def remain_one(p):
        c = u[p // 2]
        total = u[(p - 1) // 2] + c + u[(p + 1) // 2]
        rem[p] = keep1(p) * (left1[p] - d1[p] * c + spread(total))

    loop(3, 17, remain_one)

    def final_one(p):
        r = rem[p]
        box = spread(rem[p - 1] + r + rem[p + 1])
        f = z1[p] + u[p // 2] + ((CR + CA * d1[p]) * r - mask1(p) * box)
        zf1[(p - 4) * 20 : (p - 3) * 20, :] = f[4:24]

    loop(4, 16, final_one)

    rowsv[pl.ds(0, 240, stride=2), :] = zf1[...]
    rowsv[pl.ds(1, 240, stride=2), :] = zf1[...]
    v[...] = dot(rowsv[...], doubling(128, 256)).reshape(12, PY, EZ)
    for i in range(12):
        sv[i] = spread(v[i])

    mask0 = plane_mask(0, (PY, EZ), -4)
    keep0, mask0 = x_masks(mask0, 0), x_masks(mask0, 0, CA)

    def remain(i):
        p = i + 10
        at = p // 2 - 4
        other = (p - 1) // 2 - 4 if p % 2 == 0 else (p + 1) // 2 - 4
        rem0[i] = keep0(p) * (rs[i] - d0[p, 8:48, :] * v[at] + (2.0 * sv[at] + sv[other]))

    loop(0, 20, remain)

    def final(i):
        p = i + 10
        r = rem0[i]
        box = spread(rem0[i - 1] + r + rem0[i + 1])
        zf0[i] = zs[i] + v[p // 2 - 4] + ((CR + CA * d0[p, 8:48, :]) * r - mask0(p) * box)

    loop(1, 19, final)

    group = lax.broadcasted_iota(jnp.int32, (BY, BZ), 1) // 32
    acc = [None] * 9

    def apply(i):
        c = zf0[i + 2]
        q = d0[i + HX, 8:48, :] * c - spread(zf0[i + 1] + c + zf0[i + 3])
        q_own, z_own = q[4:36, :BZ], c[4:36, :BZ]
        z_core[i] = z_own
        q_core[i] = q_own
        if not first:
            for k, term in enumerate(products(r_old[i], z_old[i], q_old[i], z_own, q_own)):
                term = term[:8] + term[8:16] + (term[16:24] + term[24:])
                acc[k] = term if i == 0 else acc[k] + term
        if first:
            if i < 12:
                q_down[i] = q_own
            if i >= 4:
                q_up[i - 4] = q_own
            g, k = i // 4, i % 4
            halo = turn(q[4:36, BZ:], 32 * k - 112)
            if k:
                halo = jnp.where(group == k, halo, q_halo[g])
            q_halo[g] = halo
            if k == 3 and g < 3:
                q_down[12 + g] = halo
            if k == 3 and g > 0:
                q_up[11 + g] = halo

    loop(0, BX, apply)
    if not first:
        lane = lax.broadcasted_iota(jnp.int32, (1, 128), 1)
        row = jnp.zeros((1, 128), F32)
        for k, part in enumerate(acc):
            total = jnp.sum(jnp.sum(part, axis=0, keepdims=True), axis=1, keepdims=True)
            row = jnp.where(lane == k, total, row)
        dots[...] = jnp.broadcast_to(row[None], dots.shape)


def products(r, z, q, p, w):
    r1, z1, w1 = r - q, z - p, q - w
    return (
        r * z, z * q, r1 * z1, r1 * p + q * z1, q * p, z1 * w1, z1 * w + p * w1, p * w, z1 * q,
    )


def end_kernel(r, z, q, p, w, sums, solution_field, residual):
    last = jnp.sum(sums[...], axis=0)
    lane = lax.broadcasted_iota(jnp.int32, (1, 128), 1)
    at = lambda i: jnp.sum(jnp.where(lane == i, last, 0.0), axis=1, keepdims=True)
    rz, curve = at(0), at(1)
    alpha = rz / curve
    t = alpha - 1.0
    rz2 = at(2) - t * at(3) + t * t * at(4)
    zw = at(5) - t * at(6) + t * t * at(7)
    zq = at(8) - t * at(4)
    beta = rz2 / rz
    alpha2 = rz2 / (zw + 2.0 * beta * zq + beta * beta * curve)

    def body(i):
        zi, qi = z[i], q[i]
        solution_field[i] = alpha * zi + alpha2 * ((zi - alpha * p[i]) + beta * zi)
        residual[i] = (r[i] - alpha * qi) - alpha2 * ((qi - alpha * w[i]) + beta * qi)

    loop(0, BX, body)


def shape(*dims):
    return jax.ShapeDtypeStruct(dims, F32)


def call(kernel, outs, scratch, *args, aliases=None):
    whole = pl.BlockSpec(memory_space=pltpu.VMEM)
    return pl.pallas_call(
        kernel,
        out_shape=outs,
        in_specs=[whole] * len(args),
        out_specs=jax.tree.map(lambda _: whole, outs),
        scratch_shapes=[pltpu.VMEM(s, F32) for s in scratch],
        input_output_aliases=aliases or {},
        compiler_params=pltpu.CompilerParams(vmem_limit_bytes=24 * 1024 * 1024),
    )(*args)


def shift(value, axis, count, by):
    return lax.ppermute(value, axis, [(i, (i + by) % count) for i in range(count)])


def spread_coarse(packed):
    own = lax.all_to_all(packed, ("gx", "gz"), 0, 0)
    return shift(own, "gy", GY, 1), own, shift(own, "gy", GY, -1)


def early_call(first, *args):
    big, half, rows = shape(EX, EY, EZ), shape(20, PY, EZ), shape(MX * EY, MZ)
    outs = (big, big, half, half, rows) + ((big, rows) if first else ())
    return call(functools.partial(early_kernel, first), outs, [(MX * 24, EZ)], *args)


def pre_call(first, pieces, early, given=()):
    level1 = shape(MX, MY, MZ)
    new = (level1,) * (3 if first else 2) + (shape(GX * GZ, 16 if first else 8, 128),)
    outs = tuple(shape(*a.shape) for a in early) + new
    scratch = [(MX * 32, EZ), (MX, MY, MZ), (16, 128)]
    aliases = {len(pieces) + i: i for i in range(len(early))}
    kernel = functools.partial(pre_kernel, first)
    outs = call(kernel, outs, scratch, *pieces, *early, *given, aliases=aliases)
    kept = (*outs[2:4], *outs[-3:])
    return (outs[5], outs[7], *kept) if first else kept


def post_call(parts, kept, d0, d1, *old):
    first = not old
    scratch = [(28, 24, 256)] + [(16, 24, 256)] * 3 + [
        (128, 128), (256, 128), (10, 32, 128), (MX, MY, MZ), (240, 128),
        (480, 128), (12, PY, EZ), (12, PY, EZ), (20, PY, EZ), (20, PY, EZ),
    ]
    core = shape(BX, BY, BZ)
    kernel = functools.partial(post_kernel, first)
    if first:
        slab = shape(15, BY, BZ)
        outs = (shape(28, 24, 256), core, core, slab, slab, shape(4, BY, BZ))
        return call(kernel, outs, scratch, *parts, *kept, d0, d1)
    outs = (core, core, shape(GX * GY * GZ, 1, 128))
    return call(kernel, outs, scratch, *parts, *kept, d0, d1, *old)


def first_exchange(right_side, diagonal):
    def slab(lo, hi):
        return jnp.stack([right_side[lo:hi], diagonal[lo:hi]])

    xlo = shift(slab(BX - HX, BX), "gx", GX, 1)
    xhi = shift(slab(0, HX), "gx", GX, -1)
    edge = shape(2, EX // 5, BY, BZ)
    down, up = call(z_pack_kernel, (edge, edge), [], right_side, diagonal, xlo, xhi)
    zl = shift(up, "gz", GZ, 1)
    zr = shift(down, "gz", GZ, -1)
    edge = shape(168, 8, BZ)
    pieces = (right_side, diagonal, xlo, xhi, zl, zr)
    down, up = call(y_pack_kernel, (edge, edge), [], *pieces)
    early = early_call(True, *pieces)
    return (*pieces, shift(up, "gy", GY, 1), shift(down, "gy", GY, -1)), early


def later_exchange(d0, q, q_down, q_up, q_halo):
    xlo = shift(q_up, "gx", GX, 1)
    xhi = shift(q_down, "gx", GX, -1)
    edge = shape(75, 8, BZ)
    down, up = call(y_pack_later_kernel, (edge, edge), [], q, q_halo, xlo, xhi)
    early = early_call(False, q, q_halo, xlo, xhi, d0)
    return (q, q_halo, xlo, xhi, shift(up, "gy", GY, 1), shift(down, "gy", GY, -1)), early


def local(right_side, diagonal):
    d0, d1, *kept = pre_call(True, *first_exchange(right_side, diagonal))
    d2, z, q, *edges = post_call(spread_coarse(kept[-1]), kept[:-1], d0, d1)
    kept = pre_call(False, *later_exchange(d0, q, *edges), (d0, d1))
    p, w, dots = post_call(
        spread_coarse(kept[-1]), kept[:-1], d0, d1, d2, right_side, z, q
    )
    sums = lax.all_to_all(dots, ("gx", "gy", "gz"), 0, 0)
    core = shape(BX, BY, BZ)
    return call(end_kernel, (core, core), [], right_side, z, q, p, w, sums)


def solution(mesh):
    return jax.shard_map(
        local, mesh=mesh, in_specs=(SPEC, SPEC), out_specs=(SPEC, SPEC), check_vma=False
    )
```

```python
import functools

import jax
import jax.numpy as jnp
from jax import lax
from jax.experimental import pallas as pl
from jax.experimental.pallas import tpu as pltpu
from jax.sharding import PartitionSpec as P

GX, GY, GZ = 4, 8, 8
BX, BY, BZ = 16, 32, 128
HX, HY = 12, 12
EX, EY, EZ = BX + 2 * HX, BY + 2 * HY, 2 * BZ
MX, MR, MY, MZ = EX // 2, EY // 2, 32, BZ
PY = BY + 8
F32 = jnp.float32
SPEC = P("gx", "gy", "gz")


def cheb_two(lower, upper=58.0):
    theta, delta = (upper + lower) / 2.0, (upper - lower) / 2.0
    sigma = theta / delta
    rho = 1.0 / sigma
    after = 1.0 / (2.0 * sigma - rho)
    return (1.0 + after * rho) / theta + 2.0 * after / delta, -2.0 * after / (delta * theta)


CR, CA = cheb_two(7.0)


def spread_y(t):
    return t + pltpu.roll(t, 1, 0) + pltpu.roll(t, t.shape[0] - 1, 0)


def spread_z(t):
    return t + pltpu.roll(t, 1, 1) + pltpu.roll(t, t.shape[1] - 1, 1)


def spread(t):
    return spread_z(spread_y(t))


def flag(condition):
    return jnp.where(condition, 1.0, 0.0).astype(F32)


def places():
    return lax.axis_index("gx"), lax.axis_index("gy"), lax.axis_index("gz")


def plane_mask(level, shape, row):
    _, gy, gz = places()
    size = 1 << level
    y = lax.broadcasted_iota(jnp.int32, shape, 0) + (gy * (BY // size) + row)
    lane = lax.broadcasted_iota(jnp.int32, shape, 1)
    z = jnp.where(lane < 3 * shape[1] // 4, lane, lane - shape[1]) + gz * (BZ // size)
    return flag((y >= 0) & (y < GY * BY // size) & (z >= 0) & (z < GZ * BZ // size))


def x_masks(mask, level, scale=1.0):
    gx = places()[0]
    first, last = HX >> level, (HX + BX) >> level
    low, high = flag(gx > 0) * scale, flag(gx < GX - 1) * scale
    low, mid, high = mask * low, mask * scale, mask * high
    return lambda p: low if p < first else mid if p < last else high


def loop(first, last, body):
    for i in range(first, last):
        body(i)


def halving(rows, cols):
    a = lax.broadcasted_iota(jnp.int32, (rows, cols), 0)
    b = lax.broadcasted_iota(jnp.int32, (rows, cols), 1)
    return flag(a // 2 == b)


def doubling(rows, cols):
    a = lax.broadcasted_iota(jnp.int32, (rows, cols), 0)
    b = lax.broadcasted_iota(jnp.int32, (rows, cols), 1)
    return flag(b // 2 == a)


def dot(a, b):
    b = b.astype(jnp.bfloat16)
    hi = a.astype(jnp.bfloat16)
    a = a - hi.astype(F32)
    mid = a.astype(jnp.bfloat16)
    lo = (a - mid.astype(F32)).astype(jnp.bfloat16)
    one = functools.partial(jnp.dot, preferred_element_type=F32)
    return one(hi, b) + one(mid, b) + one(lo, b)


def turn(tile, by):
    by = by % 128
    return pltpu.roll(tile, by, 1) if by else tile


def x_plane(own, xlo, xhi, p):
    if p < HX:
        return xlo(p)
    return own(p - HX) if p < HX + BX else xhi(p - HX - BX)


def half_tile(src, base, plane):
    at = 4 * (plane % 2)
    return src[base + plane // 2, at : at + 4]


def z_place(p):
    if HX <= p < HX + BX:
        return (p - HX) // 5, (p - HX) % 5
    other = p if p < HX else p - BX
    return 4 + other // 5, other % 5


def z_tile(halves, t):
    return (halves[0], t) if t < 4 else (halves[1], t - 4)


def first_parts(a, own, xlo, xhi, zl, zr, ylo, yhi):
    base = a * 87

    def load(halves, t):
        ref, at = z_tile(halves, t)
        return ref[a, at]

    def parts(p):
        g, k = z_place(p)

        def pair(center, left, right):
            lane = lax.broadcasted_iota(jnp.int32, left.shape, 1)
            return center, jnp.where(lane < 64, turn(right, -24 * k), turn(left, 104 - 24 * k))

        whole = lambda y: pair(y[base + p], y[base + 40 + g], y[base + 49 + g])
        half = lambda y: pair(*(half_tile(y, base + 58, m) for m in (p, 40 + g, 49 + g)))
        center = x_plane(lambda i: own[i], lambda i: xlo[a, i], lambda i: xhi[a, i], p)
        if ylo is None:
            return [((12, 44), None, pair(center, load(zl, g), load(zr, g)))]
        return list(zip(ROWS, SIDES, (whole(ylo), half(ylo), half(yhi), whole(yhi))))

    return parts


def later_parts(own, halo, xlo, xhi, ylo, yhi):
    def parts(p):
        g, k = p // 4, p % 4
        pair = lambda center, side: (center, turn(side, 112 - 32 * k))
        whole = lambda y: pair(y[p], y[40 + g])
        half = lambda y: pair(half_tile(y, 50, p), half_tile(y, 50, 40 + g))
        center = x_plane(lambda i: own[i], lambda i: xlo[i], lambda i: xhi[i], p)
        side = x_plane(
            lambda i: halo[i // 4], lambda i: xlo[12 + i // 4], lambda i: xhi[12 + i // 4], p
        )
        if ylo is None:
            return [((12, 44), None, pair(center, side))]
        return list(zip(ROWS, SIDES, (whole(ylo), half(ylo), half(yhi), whole(yhi))))

    return parts


ROWS, SIDES = ((0, 8), (8, 12), (44, 48), (48, 56)), (0, 0, 1, 1)


def assemble_field(dst, parts):
    gx, gy, gz = places()
    lane = lax.broadcasted_iota(jnp.int32, (1, BZ), 1)
    side = jnp.where(lane < 64, flag(gz < GZ - 1), flag(gz > 0))
    x_low, x_high = flag(gx > 0), flag(gx < GX - 1)
    y_sides = flag(gy > 0), flag(gy < GY - 1)
    for p in range(EX):
        x = x_low if p < HX else None if p < HX + BX else x_high
        for (lo, hi), y, (center, halo) in parts(p):
            y = None if y is None else y_sides[y]
            scale = x if y is None else y if x is None else x * y
            dst[p, lo:hi, :BZ] = center if scale is None else center * scale
            dst[p, lo:hi, BZ:] = halo * (side if scale is None else side * scale)


def assemble_diagonal(dst, parts):
    for p in range(EX):
        for (lo, hi), _, (center, halo) in parts(p):
            dst[p, lo:hi, :BZ] = center + 27.0
            dst[p, lo:hi, BZ:] = halo + 27.0


def z_pack(planes, a, down, up):
    group = lax.broadcasted_iota(jnp.int32, (BY, BZ), 1) // 24
    for at in range(0, len(planes), 5):
        low = high = None
        for k, plane in enumerate(planes[at : at + 5]):
            src = plane()
            first, last = turn(src, 24 * k), turn(src, 24 * k - 104)
            low = first if k == 0 else jnp.where(group == k, first, low)
            high = last if k == 0 else jnp.where(group == k, last, high)
        down[a, at // 5] = low
        up[a, at // 5] = high


def z_pack_own_kernel(right_side, diagonal, down, up):
    for a, own in enumerate((right_side, diagonal)):
        z_pack([lambda i=i, own=own: own[i] for i in range(BX)], a, down, up)


def z_pack_halo_kernel(xlo, xhi, down, up):
    for a in range(2):
        planes = [lambda i=i, x=x, a=a: x[a, i] for x in (xlo, xhi) for i in range(HX)]
        z_pack(planes, a, down, up)


def y_rows(planes, base, down, up):
    count = len(planes)
    for m, plane in enumerate(planes):
        down[base + m] = plane(4, 12)
        up[base + m] = plane(20, 28)
        at = base + count + m // 2
        row = 4 * (m % 2)
        down[at, row : row + 4] = plane(0, 4)
        up[at, row : row + 4] = plane(28, 32)


def y_pack_kernel(right_side, diagonal, xlo, xhi, *refs):
    zl, zr, (down, up) = refs[0:2], refs[2:4], refs[4:]

    def rows(ref, *index):
        return lambda lo, hi: ref[(*index, slice(lo, hi))]

    for a, own in enumerate((right_side, diagonal)):
        planes = [
            x_plane(
                lambda i: rows(own, i), lambda i: rows(xlo, a, i), lambda i: rows(xhi, a, i), p
            )
            for p in range(EX)
        ]
        for halves in (zl, zr):
            for t in range(9):
                ref, at = z_tile(halves, t)
                planes.append(rows(ref, a, at))
        y_rows(planes, 87 * a, down, up)


def y_pack_later_kernel(own, halo, xlo, xhi, down, up):
    def rows(ref, index):
        return lambda lo, hi: ref[index, lo:hi]

    planes = [
        x_plane(lambda i: rows(own, i), lambda i: rows(xlo, i), lambda i: rows(xhi, i), p)
        for p in range(EX)
    ]
    planes += [
        x_plane(
            lambda i: rows(halo, i // 4),
            lambda i: rows(xlo, 12 + i // 4),
            lambda i: rows(xhi, 12 + i // 4),
            4 * g,
        )
        for g in range(10)
    ]
    y_rows(planes, 0, down, up)


def z_halve(rows, pairs, chunks):
    size = sum(hi - lo for lo, hi in chunks)
    narrow = dot(pairs[...], halving(EZ, MZ))
    for i in range(MX):
        at = i * size
        for lo, hi in chunks:
            rows[i * EY + lo : i * EY + hi] = narrow[at : at + hi - lo]
            at += hi - lo


def y_halve(rows, dst, scale):
    for p in range(MX):
        at = p * EY
        total = rows[pl.ds(at, MR, stride=2), :] + rows[pl.ds(at + 1, MR, stride=2), :]
        dst[p, :MR] = total * scale
        dst[p, MR:] = jnp.zeros((MY - MR, MZ), F32)


def clear_ends(pairs):
    size = pairs.shape[0] // MX
    pairs[0:size] = jnp.zeros((size, EZ), F32)
    pairs[(MX - 1) * size :] = jnp.zeros((size, EZ), F32)


MIDDLE, OUTER = ((16, 40),), ((0, 16), (40, 56))


def early_kernel(first, *refs):
    if first:
        right_side, diagonal, xlo, xhi = refs[:4]
        zl, zr = refs[4:6], refs[6:8]
        field, zfull, zs, rs, rows, d0, d_rows, pairs = refs[8:]
        assemble_field(field, first_parts(0, right_side, xlo, xhi, zl, zr, None, None))
        assemble_diagonal(d0, first_parts(1, diagonal, xlo, xhi, zl, zr, None, None))
        for i in range(MX):
            pairs[24 * i : 24 * i + 24] = d0[2 * i, 16:40] + d0[2 * i + 1, 16:40]
        z_halve(d_rows, pairs, MIDDLE)
    else:
        own, halo, xlo, xhi, d0 = refs[:5]
        field, zfull, zs, rs, rows, pairs = refs[5:]
        assemble_field(field, later_parts(own, halo, xlo, xhi, None, None))
    mask = x_masks(plane_mask(0, (PY, EZ), 8 - HY), 0, CA)
    for p in range(1, EX - 1):
        r = field[p, 8:48]
        box = spread(field[p - 1, 8:48] + r + field[p + 1, 8:48])
        z = (CR + CA * d0[p, 8:48]) * r - mask(p) * box
        zfull[p, 8:48] = z
        if 10 <= p < 30:
            zs[p - 10, 8:32] = z[8:32]

    def rest(p):
        total = zfull[p - 1, 8:48] + zfull[p, 8:48] + zfull[p + 1, 8:48]
        box = spread_z(spread_y(total)[8:32])
        left = field[p, 16:40] - d0[p, 16:40] * zfull[p, 16:40] + box
        if 10 <= p < 30:
            rs[p - 10, 8:32] = left
        return left

    clear_ends(pairs)
    for i in range(1, MX - 1):
        pairs[24 * i : 24 * i + 24] = rest(2 * i) + rest(2 * i + 1)
    z_halve(rows, pairs, MIDDLE)


def pre_kernel(first, *refs):
    if first:
        right_side, diagonal, xlo, xhi = refs[:4]
        zl, zr, (ylo, yhi) = refs[4:6], refs[6:8], refs[8:10]
        field, zfull, zs, rs, rows, d0, d_rows, d1 = refs[17:25]
        z1, left1, packed, pairs, r1, small = refs[25:]
        assemble_field(field, first_parts(0, right_side, xlo, xhi, zl, zr, ylo, yhi))
        assemble_diagonal(d0, first_parts(1, diagonal, xlo, xhi, zl, zr, ylo, yhi))
        for i in range(MX):
            at = 32 * i
            pairs[at : at + 16] = d0[2 * i, 0:16] + d0[2 * i + 1, 0:16]
            pairs[at + 16 : at + 32] = d0[2 * i, 40:56] + d0[2 * i + 1, 40:56]
        z_halve(d_rows, pairs, OUTER)
        y_halve(d_rows, d1, 0.125)
    else:
        own, halo, xlo, xhi, ylo, yhi = refs[:6]
        d0, d1 = refs[11:13]
        field, zfull, zs, rs, rows = refs[13:18]
        z1, left1, packed, pairs, r1, small = refs[18:]
        assemble_field(field, later_parts(own, halo, xlo, xhi, ylo, yhi))
    low = x_masks(plane_mask(0, (16, EZ), -HY), 0, CA)
    high = x_masks(plane_mask(0, (16, EZ), 40 - HY), 0, CA)

    def smooth(p):
        total = field[p - 1, 0:24] + field[p, 0:24] + field[p + 1, 0:24]
        box = spread_z(spread_y(total)[0:16])
        z = (CR + CA * d0[p, 0:16]) * field[p, 0:16] - low(p) * box
        zfull[p, 0:16] = z
        total = field[p - 1, 32:56] + field[p, 32:56] + field[p + 1, 32:56]
        box = spread_z(spread_y(total)[8:24])
        y = (CR + CA * d0[p, 40:56]) * field[p, 40:56] - high(p) * box
        zfull[p, 40:56] = y
        if 10 <= p < 30:
            zs[p - 10, 0:8] = z[8:16]
            zs[p - 10, 32:40] = y[0:8]

    def rest(p):
        total = zfull[p - 1, 0:24] + zfull[p, 0:24] + zfull[p + 1, 0:24]
        box = spread_z(spread_y(total)[0:16])
        a = field[p, 0:16] - d0[p, 0:16] * zfull[p, 0:16] + box
        total = zfull[p - 1, 32:56] + zfull[p, 32:56] + zfull[p + 1, 32:56]
        box = spread_z(spread_y(total)[8:24])
        b = field[p, 40:56] - d0[p, 40:56] * zfull[p, 40:56] + box
        if 10 <= p < 30:
            rs[p - 10, 0:8] = a[8:16]
            rs[p - 10, 32:40] = b[0:8]
        return a, b

    clear_ends(pairs)
    loop(1, EX - 1, smooth)
    for i in range(1, MX - 1):
        (a, b), (c, d) = rest(2 * i), rest(2 * i + 1)
        pairs[32 * i : 32 * i + 16] = a + c
        pairs[32 * i + 16 : 32 * i + 32] = b + d
    z_halve(rows, pairs, OUTER)
    y_halve(rows, r1, 0.5)
    mask1 = plane_mask(1, (MY, MZ), -HY // 2)
    keep1, mask1 = x_masks(mask1, 1), x_masks(mask1, 1, CA)

    def mask_one(p):
        r1[p] = r1[p] * keep1(p)

    loop(0, MX, mask_one)

    def smooth_one(p):
        r = r1[p]
        box = spread(r1[p - 1] + r + r1[p + 1])
        z1[p] = (CR + CA * d1[p]) * r - mask1(p) * box

    zero = jnp.zeros((MY, MZ), F32)
    for ref in (z1, left1):
        ref[0] = zero
        ref[MX - 1] = zero
    loop(1, MX - 1, smooth_one)

    def rest_one(p):
        z = z1[p]
        left1[p] = r1[p] - d1[p] * z + spread(z1[p - 1] + z + z1[p + 1])

    loop(1, MX - 1, rest_one)

    lane = lax.broadcasted_iota(jnp.int32, (MZ, 128), 0)
    col = lax.broadcasted_iota(jnp.int32, (MZ, 128), 1)

    def pack(src, scale):
        total = jnp.zeros((16, 128), F32)
        for k in range(4):
            s = src[6 + 2 * k, 6:22, :] + src[7 + 2 * k, 6:22, :]
            at = 32 * ((k + places()[2]) % 4)
            total = total + dot(s, flag((lane // 2 + at == col) & (lane < 64)))
        small[...] = total
        return (small[pl.ds(0, 8, stride=2), :] + small[pl.ds(1, 8, stride=2), :]) * scale

    tile = pack(left1, 0.5)
    if first:
        tile = jnp.concatenate([tile, pack(d1, 0.125)], axis=0)
    for i in range(GX * GZ):
        packed[i] = tile


def unpack(dst, row, mate, own, across, scales):
    odd = places()[1] % 2 == 1
    pick_low = lambda at: jnp.where(odd, mate[at], across[at])
    pick_own = lambda at: own[at]
    pick_high = lambda at: jnp.where(odd, across[at], mate[at])
    group = lax.broadcasted_iota(jnp.int32, (8, 128), 1) // 32
    for part, (src, scale) in enumerate(zip((pick_low, pick_own, pick_high), scales)):
        for bx in range(GX):
            for k in range(4):
                for h in range(2):
                    acc = None
                    for j in range(4):
                        block = src((bx * GZ + 4 * h + j, slice(row, row + 8)))
                        here = group == (j + k) % 4
                        acc = block if acc is None else jnp.where(here, block, acc)
                    acc = turn(acc, -32 * k)
                    rows = slice(8 * part, 8 * part + 8)
                    lanes = slice(128 * h, 128 * h + 128)
                    dst[6 + 4 * bx + k, rows, lanes] = acc if scale is None else acc * scale
    for p in (*range(6), *range(22, 28)):
        dst[p] = jnp.zeros((24, 256), F32)


def coarse(first, r2, d2, den, s0, s1, z2):
    gx, gy, _ = places()
    shape = (24, 256)
    row = lax.broadcasted_iota(jnp.int32, shape, 0) + (gy * 8 - 8)
    mask = flag((row >= 0) & (row < 64))
    low, high = mask * flag(gx > 0), mask * flag(gx < GX - 1)
    inside = lambda i: low if i < 6 else mask if i < 10 else high
    lane = lax.broadcasted_iota(jnp.int32, shape, 1)
    at = lambda ref, i: ref[4 * gx + i]

    def box(t):
        t = t + pltpu.roll(t, 1, 0) + pltpu.roll(t, 23, 0)
        return (
            t
            + jnp.where(lane == 0, 0.0, pltpu.roll(t, 1, 1))
            + jnp.where(lane == 255, 0.0, pltpu.roll(t, 255, 1))
        )

    theta, delta = 29.5, 28.5
    sigma = theta / delta
    rho = 1.0 / sigma
    rho1 = 1.0 / (2.0 * sigma - rho)
    rho2 = 1.0 / (2.0 * sigma - rho1)

    for i in range(2, 14):
        r = at(r2, i)
        step = r * (1.0 / theta)
        total = box(at(r2, i - 1) + r + at(r2, i + 1)) * (1.0 / theta)
        remain = inside(i) * (r - at(d2, i) * step + total)
        s0[i] = remain
        s1[i] = (rho1 * rho) * step + (2.0 * rho1 / delta) * remain
    for i in range(3, 13):
        step = s1[i]
        remain = inside(i) * (s0[i] - at(d2, i) * step + box(s1[i - 1] + step + s1[i + 1]))
        last = (rho2 * rho1) * step + (2.0 * rho2 / delta) * remain
        z2[i] = at(r2, i) * (1.0 / theta) + step + last
    for i in range(4, 12):
        y, d = z2[i], at(d2, i)
        left = at(r2, i) - d * y + box(z2[i - 1] + y + z2[i + 1])
        top = jnp.sum(left, axis=1, keepdims=True)
        if first:
            bottom = jnp.sum(d - 26.0, axis=1, keepdims=True)
            den[i - 4] = jnp.broadcast_to(bottom, (24, 128))
        shift_line = jnp.broadcast_to(top, (24, 128)) / den[i - 4]
        s0[i] = inside(i) * (y + jnp.concatenate([shift_line, shift_line], axis=1))


def post_kernel(first, *refs):
    lo, own, hi, zs, rs, z1, left1, d0, d1 = refs[:9]
    if first:
        d2, den, z_core, q_core, q_down, q_up, q_halo = refs[9:16]
    else:
        d2, den, r_old, z_old, q_old, z_core, q_core, dots = refs[9:17]
    r2, s0, s1, z2, wide, rows1, u, rem, zf1, rowsv, v, sv, rem0, zf0 = refs[-14:]
    gx, gy, gz = places()
    scales = (flag(gy > 0), None, flag(gy < GY - 1))
    unpack(r2, 0, lo, own, hi, scales)
    if first:
        unpack(d2, 8, lo, own, hi, (None, None, None))
    coarse(first, r2, d2, den, s0, s1, z2)

    lane = lax.broadcasted_iota(jnp.int32, (16, 128), 1)
    z = jnp.where(lane < 48, lane, lane - 64) + 32 * gz
    in2 = flag((z >= 0) & (z < 256) & (lane < 64))
    turned = (256 - 32 * gz) % 256
    for i in range(8):
        plane = pltpu.roll(s0[i + 4], turned, 1)[5:21]
        plane = jnp.where(lane < 48, plane[:, :128], turn(plane[:, 128:], 64))
        wide[16 * i : 16 * i + 16, :] = plane * in2
    up = dot(wide[...], doubling(128, 128))
    rows1[pl.ds(0, 128, stride=2), :] = up
    rows1[pl.ds(1, 128, stride=2), :] = up
    u[1:9] = rows1[...].reshape(8, 32, 128)

    mask1 = plane_mask(1, (MY, MZ), -HY // 2)
    keep1, mask1 = x_masks(mask1, 1), x_masks(mask1, 1, CA)

    def remain_one(p):
        c = u[p // 2]
        total = u[(p - 1) // 2] + c + u[(p + 1) // 2]
        rem[p] = keep1(p) * (left1[p] - d1[p] * c + spread(total))

    loop(3, 17, remain_one)

    def final_one(p):
        r = rem[p]
        box = spread(rem[p - 1] + r + rem[p + 1])
        f = z1[p] + u[p // 2] + ((CR + CA * d1[p]) * r - mask1(p) * box)
        zf1[(p - 4) * 20 : (p - 3) * 20, :] = f[4:24]

    loop(4, 16, final_one)

    rowsv[pl.ds(0, 240, stride=2), :] = zf1[...]
    rowsv[pl.ds(1, 240, stride=2), :] = zf1[...]
    v[...] = dot(rowsv[...], doubling(128, 256)).reshape(12, PY, EZ)
    for i in range(12):
        sv[i] = spread(v[i])

    mask0 = plane_mask(0, (PY, EZ), -4)
    keep0, mask0 = x_masks(mask0, 0), x_masks(mask0, 0, CA)

    def remain(i):
        p = i + 10
        at = p // 2 - 4
        other = (p - 1) // 2 - 4 if p % 2 == 0 else (p + 1) // 2 - 4
        rem0[i] = keep0(p) * (rs[i] - d0[p, 8:48, :] * v[at] + (2.0 * sv[at] + sv[other]))

    loop(0, 20, remain)

    def final(i):
        p = i + 10
        r = rem0[i]
        box = spread(rem0[i - 1] + r + rem0[i + 1])
        zf0[i] = zs[i] + v[p // 2 - 4] + ((CR + CA * d0[p, 8:48, :]) * r - mask0(p) * box)

    loop(1, 19, final)

    group = lax.broadcasted_iota(jnp.int32, (BY, BZ), 1) // 32
    acc = [None] * 9

    def apply(i):
        c = zf0[i + 2]
        q = d0[i + HX, 8:48, :] * c - spread(zf0[i + 1] + c + zf0[i + 3])
        q_own, z_own = q[4:36, :BZ], c[4:36, :BZ]
        z_core[i] = z_own
        q_core[i] = q_own
        if not first:
            for k, term in enumerate(products(r_old[i], z_old[i], q_old[i], z_own, q_own)):
                term = term[:8] + term[8:16] + (term[16:24] + term[24:])
                acc[k] = term if i == 0 else acc[k] + term
        if first:
            if i < 12:
                q_down[i] = q_own
            if i >= 4:
                q_up[i - 4] = q_own
            g, k = i // 4, i % 4
            halo = turn(q[4:36, BZ:], 32 * k - 112)
            if k:
                halo = jnp.where(group == k, halo, q_halo[g])
            q_halo[g] = halo
            if k == 3 and g < 3:
                q_down[12 + g] = halo
            if k == 3 and g > 0:
                q_up[11 + g] = halo

    loop(0, BX, apply)
    if not first:
        lane = lax.broadcasted_iota(jnp.int32, (1, 128), 1)
        row = jnp.zeros((1, 128), F32)
        for k, part in enumerate(acc):
            total = jnp.sum(jnp.sum(part, axis=0, keepdims=True), axis=1, keepdims=True)
            row = jnp.where(lane == k, total, row)
        dots[...] = jnp.broadcast_to(row[None], dots.shape)


def products(r, z, q, p, w):
    r1, z1, w1 = r - q, z - p, q - w
    return (
        r * z, z * q, r1 * z1, r1 * p + q * z1, q * p, z1 * w1, z1 * w + p * w1, p * w, z1 * q,
    )


def end_kernel(r, z, q, p, w, sums, solution_field, residual):
    last = jnp.sum(sums[...], axis=0)
    lane = lax.broadcasted_iota(jnp.int32, (1, 128), 1)
    at = lambda i: jnp.sum(jnp.where(lane == i, last, 0.0), axis=1, keepdims=True)
    rz, curve = at(0), at(1)
    alpha = rz / curve
    t = alpha - 1.0
    rz2 = at(2) - t * at(3) + t * t * at(4)
    zw = at(5) - t * at(6) + t * t * at(7)
    zq = at(8) - t * at(4)
    beta = rz2 / rz
    alpha2 = rz2 / (zw + 2.0 * beta * zq + beta * beta * curve)

    def body(i):
        zi, qi = z[i], q[i]
        solution_field[i] = alpha * zi + alpha2 * ((zi - alpha * p[i]) + beta * zi)
        residual[i] = (r[i] - alpha * qi) - alpha2 * ((qi - alpha * w[i]) + beta * qi)

    loop(0, BX, body)


def shape(*dims):
    return jax.ShapeDtypeStruct(dims, F32)


def call(kernel, outs, scratch, *args, aliases=None):
    whole = pl.BlockSpec(memory_space=pltpu.VMEM)
    return pl.pallas_call(
        kernel,
        out_shape=outs,
        in_specs=[whole] * len(args),
        out_specs=jax.tree.map(lambda _: whole, outs),
        scratch_shapes=[pltpu.VMEM(s, F32) for s in scratch],
        input_output_aliases=aliases or {},
        compiler_params=pltpu.CompilerParams(vmem_limit_bytes=24 * 1024 * 1024),
    )(*args)


def shift(value, axis, count, by):
    return lax.ppermute(value, axis, [(i, (i + by) % count) for i in range(count)])


def spread_coarse(packed):
    own = lax.all_to_all(packed, ("gx", "gz"), 0, 0)
    mate = lax.ppermute(own, "gy", [(i, i ^ 1) for i in range(GY)])
    across = lax.ppermute(own, "gy", [(i, (i + 2 * (i % 2) - 1) % GY) for i in range(GY)])
    return mate, own, across


def early_call(first, *args):
    big, half, rows = shape(EX, EY, EZ), shape(20, PY, EZ), shape(MX * EY, MZ)
    outs = (big, big, half, half, rows) + ((big, rows) if first else ())
    return call(functools.partial(early_kernel, first), outs, [(MX * 24, EZ)], *args)


def pre_call(first, pieces, early, given=()):
    level1 = shape(MX, MY, MZ)
    new = (level1,) * (3 if first else 2) + (shape(GX * GZ, 16 if first else 8, 128),)
    outs = tuple(shape(*a.shape) for a in early) + new
    scratch = [(MX * 32, EZ), (MX, MY, MZ), (16, 128)]
    aliases = {len(pieces) + i: i for i in range(len(early))}
    kernel = functools.partial(pre_kernel, first)
    outs = call(kernel, outs, scratch, *pieces, *early, *given, aliases=aliases)
    kept = (*outs[2:4], *outs[-3:])
    return (outs[5], outs[7], *kept) if first else kept


def post_call(parts, kept, d0, d1, *old):
    first = not old
    scratch = [(28, 24, 256)] + [(16, 24, 256)] * 3 + [
        (128, 128), (256, 128), (10, 32, 128), (MX, MY, MZ), (240, 128),
        (480, 128), (12, PY, EZ), (12, PY, EZ), (20, PY, EZ), (20, PY, EZ),
    ]
    core = shape(BX, BY, BZ)
    kernel = functools.partial(post_kernel, first)
    if first:
        slab = shape(15, BY, BZ)
        outs = (shape(28, 24, 256), shape(8, 24, 128), core, core, slab, slab, shape(4, BY, BZ))
        return call(kernel, outs, scratch, *parts, *kept, d0, d1)
    outs = (core, core, shape(GX * GY * GZ, 1, 128))
    return call(kernel, outs, scratch, *parts, *kept, d0, d1, *old)


def first_exchange(right_side, diagonal):
    def slab(lo, hi):
        return jnp.stack([right_side[lo:hi], diagonal[lo:hi]])

    xlo = shift(slab(BX - HX, BX), "gx", GX, 1)
    xhi = shift(slab(0, HX), "gx", GX, -1)
    edge = shape(2, 4, BY, BZ)
    down, up = call(z_pack_own_kernel, (edge, edge), [], right_side, diagonal)
    zl, zr = shift(up, "gz", GZ, 1), shift(down, "gz", GZ, -1)
    edge = shape(2, 5, BY, BZ)
    xlo, xhi, zl, zr = lax.optimization_barrier((xlo, xhi, zl, zr))
    down, up = call(z_pack_halo_kernel, (edge, edge), [], xlo, xhi)
    zl, zr = (zl, shift(up, "gz", GZ, 1)), (zr, shift(down, "gz", GZ, -1))
    edge = shape(174, 8, BZ)
    pieces = (right_side, diagonal, xlo, xhi, *zl, *zr)
    down, up = call(y_pack_kernel, (edge, edge), [], *pieces)
    early = early_call(True, *pieces)
    return (*pieces, shift(up, "gy", GY, 1), shift(down, "gy", GY, -1)), early


def later_exchange(d0, q, q_down, q_up, q_halo):
    xlo = shift(q_up, "gx", GX, 1)
    xhi = shift(q_down, "gx", GX, -1)
    edge = shape(75, 8, BZ)
    down, up = call(y_pack_later_kernel, (edge, edge), [], q, q_halo, xlo, xhi)
    early = early_call(False, q, q_halo, xlo, xhi, d0)
    return (q, q_halo, xlo, xhi, shift(up, "gy", GY, 1), shift(down, "gy", GY, -1)), early


def local(right_side, diagonal):
    d0, d1, *kept = pre_call(True, *first_exchange(right_side, diagonal))
    d2, den, z, q, *edges = post_call(spread_coarse(kept[-1]), kept[:-1], d0, d1)
    kept = pre_call(False, *later_exchange(d0, q, *edges), (d0, d1))
    p, w, dots = post_call(
        spread_coarse(kept[-1]), kept[:-1], d0, d1, d2, den, right_side, z, q
    )
    sums = lax.all_to_all(dots, ("gx", "gy", "gz"), 0, 0)
    core = shape(BX, BY, BZ)
    return call(end_kernel, (core, core), [], right_side, z, q, p, w, sums)


def solution(mesh):
    return jax.shard_map(
        local, mesh=mesh, in_specs=(SPEC, SPEC), out_specs=(SPEC, SPEC), check_vma=False
    )
```
